32 devices in a mesh: blk: 8 (over y, x, core), space: 4 (over z).
Axes of the slice: x: 2, y: 2, z: 4, core: 2. Of those that a mesh axis runs over, the one named last changes fastest.
Arguments:
- electrons: bfloat16 [8, 8, 2, 64, 4096], P('blk', None, None, 'space'), may hold values from -4 to 4
- holes: bfloat16 [8, 8, 2, 64, 4096], P('blk', None, None, 'space'), may hold values from -4 to 4
- pair_order: int32 [8, 2], P('blk'), may hold values from 0 to 1, each once within a row
Outputs:
- potential: float32 [8, 2, 64, 64, 128], P('blk', None, 'space')
- coulomb: float32 [8, 2, 2, 2], P('blk')
The draws below stay inside these ranges and needn't reach their ends.
Inputs may be any that keep to these rules, and one draw needn't show every extreme that they name: `pair_order`: each row lists every candidate once.
All inputs are finite; a program needn't handle non-finite values.
Results may differ from the reference program's by a relative error of at most 0.0003.
Values may be sent and summed in bfloat16 or wider, within the bound.
A program may use at most 64 MiB of HBM per device.

```python
import math
import jax
import jax.numpy as jnp
from jax import lax

BANDS = 8
NX = 64
NY = 64
NZ = 64
EG = 1
HG = 1
GROUPS = 8
E = 8
H = 8
P_SIZE = 2


def dot_envelopes(key, amount):
    keys = jax.random.split(key, 5)
    centre_x = jax.random.uniform(keys[0], (amount,), jnp.float32, 0.3, 0.7)
    centre_y = jax.random.uniform(keys[1], (amount,), jnp.float32, 0.3, 0.7)
    upper_dot = jax.random.randint(keys[2], (amount,), 0, 2).astype(jnp.float32)
    centre_z = 0.35 + 0.3 * upper_dot + jax.random.uniform(keys[3], (amount,), jnp.float32, -0.05, 0.05)
    spread = jax.random.uniform(keys[4], (amount,), jnp.float32, 0.12, 0.25)
    grid_x = (jnp.arange(NX, dtype=jnp.float32) + 0.5) / NX
    grid_y = (jnp.arange(NY, dtype=jnp.float32) + 0.5) / NY
    grid_z = (jnp.arange(NZ, dtype=jnp.float32) + 0.5) / NZ
    distance = (grid_x[None, :, None, None] - centre_x[:, None, None, None]) ** 2
    distance = distance + (grid_y[None, None, :, None] - centre_y[:, None, None, None]) ** 2
    distance = distance + (grid_z[None, None, None, :] - centre_z[:, None, None, None]) ** 2
    envelope = jnp.exp(-distance / (2.0 * spread[:, None, None, None] ** 2))
    return envelope.reshape(amount, NX, NY * NZ)


def draw_states(key, amount, salt):
    own_key = jax.random.fold_in(key, salt)
    keys = jax.random.split(own_key, 3)
    envelope = dot_envelopes(keys[0], amount)
    amplitude = jax.random.normal(keys[1], (amount, BANDS, 2, 1, 1), jnp.float32)
    rough = jax.random.normal(keys[2], (amount, BANDS, 2, NX, NY * NZ), jnp.float32)
    scaling = jnp.ones((amount, 1, 1, 1, 1), jnp.float32)
    modulated = (0.2 + envelope[:, None, None]) * amplitude
    spread = jnp.sqrt(modulated * modulated + 0.36)
    states = 0.25 * scaling * rough * spread
    return jnp.clip(states, -4.0, 4.0).astype(jnp.bfloat16)


def draw_electrons(key, part):
    return draw_states(key, E, 11)


def draw_holes(key, part):
    return draw_states(key, H, 12)


def setup_inputs(seed: int = 0) -> dict:
    arg_keys = jax.random.split(jax.random.key(seed), 4)
    return {
        "electrons": draw_electrons(jax.random.fold_in(arg_keys[3], 71), 0),
        "holes": draw_holes(jax.random.fold_in(arg_keys[3], 71), 0),
        "pair_order": jax.vmap(lambda own: jax.random.permutation(own, P_SIZE))(jax.random.split(arg_keys[2], GROUPS)).reshape((GROUPS, P_SIZE)).astype(jnp.int32),
    }


SCREENING = 0.01


def lattice_term(indices, points):
    return 2.0 - 2.0 * jnp.cos((2.0 * math.pi / points) * (indices % points).astype(jnp.float32))


def reference(electrons, holes, pair_order):
    index_x = jnp.arange(NX, dtype=jnp.int32)
    index_y = jnp.arange(NY, dtype=jnp.int32)
    index_z = jnp.arange(NZ, dtype=jnp.int32)
    term_x = lattice_term(index_x, NX)
    term_y = lattice_term(index_y, NY)
    term_z = lattice_term(index_z, NZ)
    green = 1.0 / (term_x[:, None, None] + term_y[None, :, None] + term_z[None, None, :] + SCREENING)
    anchor = (index_x[:, None, None] == 0) & (index_y[None, :, None] == 0) & (index_z[None, None, :] == 0)
    green = jnp.where(anchor, jnp.zeros_like(green), green)
    cells = NX * NY * NZ

    def banded(first_set, second_set):
        return jnp.einsum("ebxc,hbxc->hexc", first_set, second_set, precision=lax.Precision.HIGHEST)

    def one_group(group):
        group = group.astype(jnp.int32)
        prior = jnp.mod(group - 1 + GROUPS, GROUPS).astype(jnp.int32)
        elec = lax.dynamic_slice_in_dim(electrons, (group * EG).astype(jnp.int32), EG, 0).astype(jnp.float32)
        hole_own = lax.dynamic_slice_in_dim(holes, (group * HG).astype(jnp.int32), HG, 0)
        hole_far = lax.dynamic_slice_in_dim(holes, (prior * HG).astype(jnp.int32), HG, 0)
        hole_set = jnp.concatenate([hole_own, hole_far], axis=0).astype(jnp.float32)
        real_part = banded(elec[:, :, 0], hole_set[:, :, 0]) + banded(elec[:, :, 1], hole_set[:, :, 1])
        imag_part = banded(elec[:, :, 0], hole_set[:, :, 1]) - banded(elec[:, :, 1], hole_set[:, :, 0])
        target_shape = (P_SIZE, NX, NY, NZ)
        densities = lax.complex(real_part.reshape(target_shape), imag_part.reshape(target_shape))
        spectra = jnp.fft.fftn(densities, axes=(1, 2, 3))
        field = jnp.fft.ifftn(spectra * green[None], axes=(1, 2, 3))
        pair_rank = pair_order[group]
        field = jnp.take(field, pair_rank, axis=0)
        densities = jnp.take(densities, pair_rank, axis=0)
        flat_field = field.reshape(P_SIZE, -1)
        flat_dens = jnp.conj(densities.reshape(P_SIZE, -1))
        product = jnp.einsum("pn,qn->pq", flat_field, flat_dens, precision=lax.Precision.HIGHEST) / cells
        potential = jnp.concatenate([jnp.real(field), jnp.imag(field)], axis=-1)
        coulomb = jnp.stack([jnp.real(product), jnp.imag(product)])
        return potential, coulomb

    potential, coulomb = lax.map(one_group, jnp.arange(GROUPS, dtype=jnp.int32))
    return potential, coulomb
```

```python
import functools
import math

import jax
import jax.numpy as jnp
import numpy as np
from jax import lax
from jax.experimental import pallas as pl
from jax.experimental.pallas import tpu as pltpu
from jax.sharding import PartitionSpec as P

SCREENING = 0.01
MESH = pl.DeviceIdType.MESH
LANES = 128
CHUNK = 8
F32 = jnp.float32
BF16 = jnp.bfloat16


def halves(matrix):
    high = matrix.astype(jnp.bfloat16)
    low = (matrix - high.astype(np.float64)).astype(jnp.bfloat16)
    return high, low


def phases(points):
    positions = np.arange(points)
    angles = 2.0 * math.pi / points * (np.outer(positions, positions) % points)
    return np.cos(angles), np.sin(angles)


def depth_table(points, direction):
    cosines, sines = phases(points)
    sines = direction * sines
    matrix = np.concatenate(
        [np.concatenate([cosines, -sines], 1), np.concatenate([sines, cosines], 1)], 0
    )
    high, low = halves(matrix)
    top = np.concatenate([high, low], 1)
    bottom = np.concatenate([high, np.zeros_like(high)], 1)
    return np.concatenate([top, bottom], 0)


def column_table(points, direction):
    cosines, sines = phases(points)
    high, low = halves(np.concatenate([cosines, direction * sines], 1))
    top = np.concatenate([high, high], 1)
    bottom = np.concatenate([low, np.zeros_like(low)], 1)
    return np.concatenate([top, bottom], 0)


def chunk_table(points):
    cosines, sines = phases(points)
    tables = []
    for start in range(0, points, CHUNK):
        own = slice(start, start + CHUNK)
        high, low = halves(np.concatenate([cosines[:, own], sines[:, own]], 1))
        fill = np.zeros((points, LANES - 6 * CHUNK), high.dtype)
        tables.append(np.concatenate([high, high, low, fill], 1))
    return np.stack(tables)


def solver_tables(nx, ny, nz, devices):
    term_y = 2.0 - 2.0 * np.cos(2.0 * math.pi / ny * np.arange(ny))
    term_z = 2.0 - 2.0 * np.cos(2.0 * math.pi / nz * (np.arange(2 * nz) % nz))
    shift = term_y[:, None] + term_z[None, :] + SCREENING
    root = np.sqrt(shift * (shift + 4.0))
    decay = 2.0 / (shift + 2.0 + root)
    response = 1.0 / root / (ny * nz)
    anchor = np.zeros_like(shift)
    anchor[0, 0] = anchor[0, nz] = 1.0 / (SCREENING * nx * ny * nz)
    rows = nx // devices
    weights = [decay ** (rows * j) / (1.0 - decay**nx) for j in range(devices)]
    return np.stack([decay, response, anchor] + weights).astype(np.float32)


def split(values):
    high = values.astype(BF16)
    return high, (values - high.astype(F32)).astype(BF16)


def turned(values, sign):
    return pltpu.roll(values, LANES // 2, values.ndim - 1) * sign


def sign_of(lane):
    return jnp.where(lane < LANES // 2, 1.0, -1.0).astype(F32)


def inverse(values, z_ref, y_ref, ny, sign):
    planes = values.shape[0] // ny
    high, low = split(values)
    wide = jnp.dot(jnp.concatenate([high, low], 1), z_ref[...], preferred_element_type=F32)
    deep = wide[:, :LANES] + wide[:, LANES:]
    turn = turned(deep, sign)
    high, low = split(deep)
    turn_high, turn_low = split(turn)
    parts = []
    for x in range(0, planes, 2):
        columns = []
        for k in (x, x + 1):
            own = slice(k * ny, (k + 1) * ny)
            columns.append(
                jnp.concatenate([high[own], turn_high[own], low[own], turn_low[own]], 0)
            )
        both = jnp.dot(y_ref[...], jnp.concatenate(columns, 1), preferred_element_type=F32)
        total = both[:ny] + both[ny:]
        parts += [total[:, :LANES], total[:, LANES:]]
    return jnp.concatenate(parts, 0)


def kernel(
    n, blocks, ny,
    e_hbm, h_hbm, zf_hbm, chunk_hbm, back_hbm, tab_hbm,
    res_ref, out_ref, sum_ref, back_ref,
    e_ref, h_ref, prev_ref, stage_ref, rho_ref, fld_ref, msg_ref, recv_ref,
    part_ref, peer_ref, far_ref, zf_ref, chunk_ref, tab_ref,
    load_sem, hole_send, hole_recv, msg_send, msg_recv, part_send, part_recv,
):
    bands, _, rows, cells = e_ref.shape
    chunks = ny // CHUNK
    wide = cells // chunks
    group = lax.axis_index("blk")
    me = lax.axis_index("space")
    following = lax.rem(group + 1, blocks)
    preceding = lax.rem(group + blocks - 1, blocks)
    others = [lax.rem(me + j, n) for j in range(1, n)]

    loads = [
        pltpu.make_async_copy(e_hbm.at[0], e_ref, load_sem.at[0]),
        pltpu.make_async_copy(h_hbm.at[0], h_ref, load_sem.at[1]),
        pltpu.make_async_copy(zf_hbm, zf_ref, load_sem.at[2]),
        pltpu.make_async_copy(chunk_hbm, chunk_ref, load_sem.at[3]),
        pltpu.make_async_copy(back_hbm, back_ref, load_sem.at[4]),
        pltpu.make_async_copy(tab_hbm, tab_ref, load_sem.at[5]),
    ]
    zi_ref = back_ref.at[0 : 2 * LANES]
    yi_ref = back_ref.at[2 * LANES : 3 * LANES]
    for copy in loads:
        copy.start()

    barrier = pltpu.get_barrier_semaphore()
    for neighbour in (following, preceding):
        pl.semaphore_signal(barrier, inc=1, device_id=(neighbour, me), device_id_type=MESH)
    for other in others:
        pl.semaphore_signal(barrier, inc=1, device_id=(group, other), device_id_type=MESH)
    pl.semaphore_wait(barrier, n + 1)

    def hole_copy(k):
        window = pl.ds(pl.multiple_of(k * wide, wide), wide)
        return pltpu.make_async_remote_copy(
            src_ref=h_hbm.at[0, :, :, :, window], dst_ref=prev_ref.at[:, :, :, window],
            send_sem=hole_send.at[k], recv_sem=hole_recv.at[k],
            device_id=(following, me), device_id_type=MESH,
        )

    for k in range(chunks):
        hole_copy(k).start()

    lane = lax.broadcasted_iota(jnp.int32, (1, LANES), 1)
    first_half = lane < LANES // 2
    sign = sign_of(lane)

    def products(holes, t):
        window = pl.ds(pl.multiple_of(t * LANES, LANES), LANES)
        real = imag = None
        for b in range(bands):
            er = e_ref[b, 0, :, window].astype(F32)
            ei = e_ref[b, 1, :, window].astype(F32)
            hr = holes[b, 0, :, window].astype(F32)
            hi = holes[b, 1, :, window].astype(F32)
            if b == 0:
                real, imag = er * hr + ei * hi, er * hi - ei * hr
            else:
                real = real + (er * hr + ei * hi)
                imag = imag + (er * hi - ei * hr)
        return real, imag

    def clear(c):
        @pl.loop(0, rows)
        def _(x):
            rho_ref[c, pl.ds(pl.multiple_of(x * ny, ny), ny), :] = jnp.zeros((ny, LANES), F32)

    def absorb(c, holes, k):
        for t in range(wide // LANES):
            real, imag = products(holes, k * (wide // LANES) + t)
            moved_real = pltpu.roll(real, LANES // 2, 1)
            moved_imag = pltpu.roll(imag, LANES // 2, 1)
            stage_ref[pl.ds(2 * t, rows, stride=CHUNK), :] = jnp.where(
                first_half, real, moved_imag
            )
            stage_ref[pl.ds(2 * t + 1, rows, stride=CHUNK), :] = jnp.where(
                first_half, moved_real, imag
            )
        high, low = split(stage_ref[...])
        both = jnp.dot(
            jnp.concatenate([high, low], 1), zf_ref[...], preferred_element_type=F32
        )
        deep = both[:, :LANES] + both[:, LANES:]
        turn = turned(deep, sign)
        table = chunk_ref[k][:, : 6 * CHUNK]
        for x in range(0, rows, 2):
            pair = []
            for j in (x, x + 1):
                own = slice(j * CHUNK, (j + 1) * CHUNK)
                pair.append(jnp.concatenate([deep[own], turn[own]], 0))
            high, low = split(jnp.concatenate(pair, 1))
            share = jnp.dot(
                table, jnp.concatenate([high, low, high], 0), preferred_element_type=F32
            )
            for j in range(2):
                own = slice((x + j) * ny, (x + j + 1) * ny)
                rho_ref[c, own, :] = rho_ref[c, own, :] + share[:, j * LANES : (j + 1) * LANES]

    planes = min(rows, 4)
    span = planes * ny
    block = 16

    fields = [fld_ref, out_ref]

    def moments(c):
        @pl.loop(0, ny // block, unroll=2)
        def _(i):
            at = pl.multiple_of(i * block, block)
            decay = tab_ref[0, pl.ds(at, block), :]
            left = jnp.zeros((block, LANES), F32)
            right = jnp.zeros((block, LANES), F32)
            for x in range(rows):
                left = decay * left + rho_ref[c, pl.ds(x * ny + at, block), :]
                y = rows - 1 - x
                right = decay * right + rho_ref[c, pl.ds(y * ny + at, block), :]
            msg_ref[c, pl.ds(at, block), :] = left
            msg_ref[c, pl.ds(ny + at, block), :] = right

        total = rho_ref[c, 0:8, :]
        for x in range(1, rows):
            total = total + rho_ref[c, x * ny : x * ny + 8, :]
        msg_ref[c, 2 * ny : 2 * ny + 8, :] = total
        copies = [
            pltpu.make_async_remote_copy(
                src_ref=msg_ref.at[c], dst_ref=recv_ref.at[c, j],
                send_sem=msg_send.at[c, j], recv_sem=msg_recv.at[c, j],
                device_id=(group, others[j]), device_id_type=MESH,
            )
            for j in range(n - 1)
        ]
        for copy in copies:
            copy.start()
        return copies

    empty = jnp.zeros((block, LANES), F32)

    def local(c):
        def body(i, energy):
            at = pl.multiple_of(i * block, block)
            decay = tab_ref[0, pl.ds(at, block), :]
            response = tab_ref[1, pl.ds(at, block), :]
            left = right = empty
            spread = []
            for x in reversed(range(rows)):
                right = decay * right
                spread.append(right)
                right = right + rho_ref[c, pl.ds(x * ny + at, block), :]
            for x in range(rows):
                value = rho_ref[c, pl.ds(x * ny + at, block), :]
                left = decay * left + value
                field = response * (left + spread[rows - 1 - x])
                fields[c][pl.ds(x * ny + at, block), :] = field
                energy = energy + field * value
            return energy

        total = lax.fori_loop(0, ny // block, body, empty)
        return jnp.sum(total, axis=0, keepdims=True)

    def solve(c):
        mean = msg_ref[c, 2 * ny : 2 * ny + 8, :]
        for k in range(n - 1):
            mean = mean + recv_ref[c, k, 2 * ny : 2 * ny + 8, :]
        mean = jnp.concatenate([mean, mean], 0)

        def body(i, energy):
            at = pl.multiple_of(i * block, block)
            decay = tab_ref[0, pl.ds(at, block), :]
            response = tab_ref[1, pl.ds(at, block), :]
            background = tab_ref[2, pl.ds(at, block), :] * mean
            weights = [tab_ref[3 + k, pl.ds(at, block), :] for k in range(n)]
            rights = [msg_ref[c, pl.ds(at, block), :]]
            lefts = [msg_ref[c, pl.ds(ny + at, block), :]]
            for k in range(n - 1):
                rights.append(recv_ref[c, k, pl.ds(at, block), :])
                lefts.append(recv_ref[c, k, pl.ds(ny + at, block), :])
            left = right = pairs = empty
            for a in range(n):
                coming = empty
                for k in range(n):
                    coming = coming + weights[k] * rights[(a + k + 1) % n]
                pairs = pairs + coming * lefts[a]
                if a == 0:
                    left = coming
            for k in range(n):
                right = right + weights[k] * lefts[(n - k - 1) % n]
            energy = energy + 2.0 * response * decay * pairs - background * mean
            left = response * left
            right = response * right
            spread = []
            for x in range(rows):
                right = decay * right
                spread.append(right)
            for x in range(rows):
                left = decay * left
                own = pl.ds(x * ny + at, block)
                fields[c][own, :] = fields[c][own, :] + (
                    left + spread[rows - 1 - x] - background
                )
            return energy

        total = lax.fori_loop(0, ny // block, body, empty)
        return jnp.sum(total, axis=0, keepdims=True)

    for copy in loads:
        copy.wait()

    clear(0)
    clear(1)

    @pl.loop(0, chunks)
    def _(k):
        absorb(0, h_ref, k)

    copies0 = moments(0)
    part_ref[0:1, :] = local(0)

    early = min(chunks, 2)

    @pl.loop(0, early)
    def _(k):
        hole_copy(k).wait_recv()
        absorb(1, prev_ref, k)

    for copy in copies0:
        copy.wait_recv()
    far_ref[0:1, :] = solve(0)

    @pl.loop(0, rows // planes)
    def _(i):
        own = pl.ds(pl.multiple_of(i * span, span), span)
        res_ref[own, :] = inverse(fld_ref[own, :], zi_ref, yi_ref, ny, sign)

    @pl.loop(early, chunks)
    def _(k):
        hole_copy(k).wait_recv()
        absorb(1, prev_ref, k)

    copies1 = moments(1)
    part_ref[1:2, :] = local(1)

    def cross(i, sums):
        at = pl.ds(pl.multiple_of(i * block, block), block)
        field = fld_ref[at, :]
        value = rho_ref[1, at, :]
        return sums[0] + field * value, sums[1] - field * turned(value, sign)

    real, imag = lax.fori_loop(0, rows * ny // block, cross, (empty, empty), unroll=4)
    part_ref[2:3, :] = jnp.sum(real, axis=0, keepdims=True)
    part_ref[3:4, :] = jnp.sum(imag, axis=0, keepdims=True)
    part_ref[4:8, :] = jnp.zeros((4, LANES), F32)
    far_ref[2:8, :] = jnp.zeros((6, LANES), F32)
    part_copies = [
        pltpu.make_async_remote_copy(
            src_ref=part_ref, dst_ref=peer_ref.at[j],
            send_sem=part_send.at[j], recv_sem=part_recv.at[j],
            device_id=(group, others[j]), device_id_type=MESH,
        )
        for j in range(n - 1)
    ]
    for copy in part_copies:
        copy.start()

    for copy in copies1:
        copy.wait_recv()
    far_ref[1:2, :] = solve(1)

    for copy in part_copies:
        copy.wait_recv()
    total = part_ref[...] + far_ref[...]
    for j in range(n - 1):
        total = total + peer_ref[j]
    sum_ref[...] = total

    for copy in [hole_copy(k) for k in range(chunks)] + copies0 + copies1 + part_copies:
        copy.wait_send()


def finish(
    ny, scale, order_ref, res_ref, fld_ref, sum_ref, back_ref,
    out_hbm, coul_ref, stage_ref, out_sem,
):
    flat = res_ref.shape[0]
    first, second = order_ref[0, 0], order_ref[0, 1]
    stored = pltpu.make_async_copy(res_ref, out_hbm.at[first], out_sem.at[0])
    stored.start()
    sign = sign_of(lax.broadcasted_iota(jnp.int32, (1, LANES), 1))
    span = min(flat // ny, 4) * ny
    copies = [stored]
    for i in range(flat // span):
        own = slice(i * span, (i + 1) * span)
        stage_ref[own, :] = inverse(
            fld_ref[own, :], back_ref.at[0 : 2 * LANES], back_ref.at[2 * LANES : 3 * LANES],
            ny, sign,
        )
        copy = pltpu.make_async_copy(
            stage_ref.at[own], out_hbm.at[1 - first, own], out_sem.at[i + 1]
        )
        copy.start()
        copies.append(copy)

    entries = [jnp.sum(sum_ref[k : k + 1, :]) * scale for k in range(4)]
    shape = (2, 2, 2)
    part_of = lax.broadcasted_iota(jnp.int32, shape, 0)
    row = lax.broadcasted_iota(jnp.int32, shape, 1)
    column = lax.broadcasted_iota(jnp.int32, shape, 2)
    row_pair = jnp.where(row == 0, first, second)
    column_pair = jnp.where(column == 0, first, second)
    same = row_pair == column_pair
    opening = row_pair == 0
    real = jnp.where(same, jnp.where(opening, entries[0], entries[1]), entries[2])
    imag = jnp.where(same, 0.0, jnp.where(opening, entries[3], -entries[3]))
    coul_ref[0] = jnp.where(part_of == 0, real, imag)
    for copy in copies:
        copy.wait()


def shards(n, blocks, electrons, holes, pair_order):
    _, bands, parts, rows, cells = electrons.shape
    ny = nz = math.isqrt(cells)
    flat = rows * ny
    nx = rows * n
    vmem = pl.BlockSpec(memory_space=pltpu.VMEM)
    hbm = pl.BlockSpec(memory_space=pl.ANY)
    states = (bands, parts, rows, cells)
    message = 2 * ny + 8
    chunks = ny // CHUNK
    back = np.concatenate([depth_table(nz, -1.0), column_table(ny, -1.0)])
    tables = solver_tables(nx, ny, nz, n)
    stored, field, sums, back_kept = pl.pallas_call(
        functools.partial(kernel, n, blocks, ny),
        out_shape=(
            pltpu.VMEM((flat, LANES), F32),
            pltpu.VMEM((flat, LANES), F32),
            pltpu.VMEM((8, LANES), F32),
            pltpu.VMEM(back.shape, BF16),
        ),
        in_specs=[hbm] * 6,
        out_specs=(vmem,) * 4,
        scratch_shapes=[
            pltpu.VMEM(states, BF16),
            pltpu.VMEM(states, BF16),
            pltpu.VMEM(states, BF16),
            pltpu.VMEM((rows * CHUNK, LANES), F32),
            pltpu.VMEM((2, flat, LANES), F32),
            pltpu.VMEM((flat, LANES), F32),
            pltpu.VMEM((2, message, LANES), F32),
            pltpu.VMEM((2, n - 1, message, LANES), F32),
            pltpu.VMEM((8, LANES), F32),
            pltpu.VMEM((n - 1, 8, LANES), F32),
            pltpu.VMEM((8, LANES), F32),
            pltpu.VMEM((2 * LANES, 2 * LANES), BF16),
            pltpu.VMEM((chunks, ny, LANES), BF16),
            pltpu.VMEM(tables.shape, F32),
            pltpu.SemaphoreType.DMA((6,)),
            pltpu.SemaphoreType.DMA((chunks,)),
            pltpu.SemaphoreType.DMA((chunks,)),
            pltpu.SemaphoreType.DMA((2, n - 1)),
            pltpu.SemaphoreType.DMA((2, n - 1)),
            pltpu.SemaphoreType.DMA((n - 1,)),
            pltpu.SemaphoreType.DMA((n - 1,)),
        ],
        compiler_params=pltpu.CompilerParams(
            collective_id=0, has_side_effects=True, vmem_limit_bytes=60 * 2**20
        ),
        name="screened",
    )(
        electrons,
        holes,
        jnp.asarray(depth_table(nz, 1.0)),
        jnp.asarray(chunk_table(ny)),
        jnp.asarray(back),
        jnp.asarray(tables),
    )
    potential, coulomb = pl.pallas_call(
        functools.partial(finish, ny, 1.0 / (nx * cells)),
        out_shape=(
            jax.ShapeDtypeStruct((2, flat, LANES), F32),
            jax.ShapeDtypeStruct((1, 2, 2, 2), F32),
        ),
        in_specs=[pl.BlockSpec(memory_space=pltpu.SMEM), vmem, vmem, vmem, vmem],
        out_specs=(hbm, vmem),
        scratch_shapes=[
            pltpu.VMEM((flat, LANES), F32),
            pltpu.SemaphoreType.DMA((1 + flat // (min(rows, 4) * ny),)),
        ],
        compiler_params=pltpu.CompilerParams(vmem_limit_bytes=16 * 2**20),
        name="finish",
    )(pair_order, stored, field, sums, back_kept)
    return potential.reshape(1, 2, rows, ny, 2 * nz), coulomb


def solution(mesh):
    body = functools.partial(shards, mesh.shape["space"], mesh.shape["blk"])
    in_specs = (
        P("blk", None, None, "space", None),
        P("blk", None, None, "space", None),
        P("blk", None),
    )
    out_specs = (P("blk", None, "space", None, None), P("blk", None, None, None))
    return jax.shard_map(body, mesh=mesh, in_specs=in_specs, out_specs=out_specs, check_vma=False)
```

```python
import functools
import math

import jax
import jax.numpy as jnp
import numpy as np
from jax import lax
from jax.experimental import pallas as pl
from jax.experimental.pallas import tpu as pltpu
from jax.sharding import PartitionSpec as P

SCREENING = 0.01
MESH = pl.DeviceIdType.MESH
LANES = 128
CHUNK = 8
F32 = jnp.float32
BF16 = jnp.bfloat16


def halves(matrix):
    high = matrix.astype(jnp.bfloat16)
    low = (matrix - high.astype(np.float64)).astype(jnp.bfloat16)
    return high, low


def phases(points):
    positions = np.arange(points)
    angles = 2.0 * math.pi / points * (np.outer(positions, positions) % points)
    return np.cos(angles), np.sin(angles)


def depth_table(points, direction):
    cosines, sines = phases(points)
    sines = direction * sines
    matrix = np.concatenate(
        [np.concatenate([cosines, -sines], 1), np.concatenate([sines, cosines], 1)], 0
    )
    high, low = halves(matrix)
    top = np.concatenate([high, low], 1)
    bottom = np.concatenate([high, np.zeros_like(high)], 1)
    return np.concatenate([top, bottom], 0)


def column_table(points, direction):
    cosines, sines = phases(points)
    high, low = halves(np.concatenate([cosines, direction * sines], 1))
    top = np.concatenate([high, high], 1)
    bottom = np.concatenate([low, np.zeros_like(low)], 1)
    return np.concatenate([top, bottom], 0)


def chunk_table(points):
    cosines, sines = phases(points)
    tables = []
    for start in range(0, points, CHUNK):
        own = slice(start, start + CHUNK)
        high, low = halves(np.concatenate([cosines[:, own], sines[:, own]], 1))
        fill = np.zeros((points, LANES - 6 * CHUNK), high.dtype)
        tables.append(np.concatenate([high, high, low, fill], 1))
    return np.stack(tables)


def solver_tables(nx, ny, nz, devices):
    term_y = 2.0 - 2.0 * np.cos(2.0 * math.pi / ny * np.arange(ny))
    term_z = 2.0 - 2.0 * np.cos(2.0 * math.pi / nz * (np.arange(2 * nz) % nz))
    shift = term_y[:, None] + term_z[None, :] + SCREENING
    root = np.sqrt(shift * (shift + 4.0))
    decay = 2.0 / (shift + 2.0 + root)
    response = 1.0 / root / (ny * nz)
    anchor = np.zeros_like(shift)
    anchor[0, 0] = anchor[0, nz] = 1.0 / (SCREENING * nx * ny * nz)
    rows = nx // devices
    weights = [decay ** (rows * j) / (1.0 - decay**nx) for j in range(devices)]
    return np.stack([decay, response, anchor] + weights).astype(np.float32)


def split(values):
    high = values.astype(BF16)
    return high, (values - high.astype(F32)).astype(BF16)


def turned(values, sign):
    return pltpu.roll(values, LANES // 2, values.ndim - 1) * sign


def sign_of(lane):
    return jnp.where(lane < LANES // 2, 1.0, -1.0).astype(F32)


def inverse(values, z_ref, y_ref, ny, sign):
    planes = values.shape[0] // ny
    high, low = split(values)
    wide = jnp.dot(jnp.concatenate([high, low], 1), z_ref[...], preferred_element_type=F32)
    deep = wide[:, :LANES] + wide[:, LANES:]
    turn = turned(deep, sign)
    high, low = split(deep)
    turn_high, turn_low = split(turn)
    parts = []
    for x in range(0, planes, 2):
        columns = []
        for k in (x, x + 1):
            own = slice(k * ny, (k + 1) * ny)
            columns.append(
                jnp.concatenate([high[own], turn_high[own], low[own], turn_low[own]], 0)
            )
        both = jnp.dot(y_ref[...], jnp.concatenate(columns, 1), preferred_element_type=F32)
        total = both[:ny] + both[ny:]
        parts += [total[:, :LANES], total[:, LANES:]]
    return jnp.concatenate(parts, 0)


def kernel(
    n, blocks, ny,
    e_hbm, h_hbm, zf_hbm, chunk_hbm, back_hbm, tab_hbm,
    res_ref, out_ref, sum_ref, back_ref,
    e_ref, h_ref, prev_ref, stage_ref, rho_ref, fld_ref, msg_ref, recv_ref,
    turn_ref, zf_ref, chunk_ref, tab_ref,
    load_sem, hole_send, hole_recv, msg_send, msg_recv, greet_sem, ready_sem,
):
    bands, _, rows, cells = e_ref.shape
    chunks = ny // CHUNK
    wide = cells // chunks
    group = lax.axis_index("blk")
    me = lax.axis_index("space")
    following = lax.rem(group + 1, blocks)
    preceding = lax.rem(group + blocks - 1, blocks)
    others = [j + (me <= j).astype(jnp.int32) for j in range(n - 1)]

    loads = [
        pltpu.make_async_copy(e_hbm.at[0], e_ref, load_sem.at[0]),
        pltpu.make_async_copy(h_hbm.at[0], h_ref, load_sem.at[1]),
        pltpu.make_async_copy(zf_hbm, zf_ref, load_sem.at[2]),
        pltpu.make_async_copy(chunk_hbm, chunk_ref, load_sem.at[3]),
        pltpu.make_async_copy(back_hbm, back_ref, load_sem.at[4]),
        pltpu.make_async_copy(tab_hbm, tab_ref, load_sem.at[5]),
    ]
    zi_ref = back_ref.at[0 : 2 * LANES]
    yi_ref = back_ref.at[2 * LANES : 3 * LANES]
    for copy in loads:
        copy.start()

    even = lax.rem(group, 2) == 0
    barrier = pltpu.get_barrier_semaphore()
    pl.semaphore_signal(barrier, inc=1, device_id=(preceding, me), device_id_type=MESH)

    @pl.when(even)
    def _():
        for other in others:
            pl.semaphore_signal(barrier, inc=1, device_id=(group, other), device_id_type=MESH)

    pl.semaphore_wait(barrier, jnp.where(even, n, 1))

    part = wide // 2

    def hole_copy(k):
        window = pl.ds(pl.multiple_of(k * part, part), part)
        return pltpu.make_async_remote_copy(
            src_ref=h_hbm.at[0, :, :, :, window], dst_ref=prev_ref.at[:, :, :, window],
            send_sem=hole_send.at[k], recv_sem=hole_recv.at[k],
            device_id=(following, me), device_id_type=MESH,
        )

    for k in range(2 * chunks):
        hole_copy(k).start()

    @pl.when(even)
    def _():
        for other in others:
            pl.semaphore_signal(greet_sem, inc=1, device_id=(group, other), device_id_type=MESH)
        pl.semaphore_wait(greet_sem, n - 1)
        pl.semaphore_signal(ready_sem, inc=1, device_id=(following, me), device_id_type=MESH)

    lane = lax.broadcasted_iota(jnp.int32, (1, LANES), 1)
    first_half = lane < LANES // 2
    sign = sign_of(lane)

    def products(holes, t):
        window = pl.ds(pl.multiple_of(t * LANES, LANES), LANES)
        real = imag = None
        for b in range(bands):
            er = e_ref[b, 0, :, window].astype(F32)
            ei = e_ref[b, 1, :, window].astype(F32)
            hr = holes[b, 0, :, window].astype(F32)
            hi = holes[b, 1, :, window].astype(F32)
            if b == 0:
                real, imag = er * hr + ei * hi, er * hi - ei * hr
            else:
                real = real + (er * hr + ei * hi)
                imag = imag + (er * hi - ei * hr)
        return real, imag

    def clear(c):
        @pl.loop(0, rows)
        def _(x):
            rho_ref[c, pl.ds(pl.multiple_of(x * ny, ny), ny), :] = jnp.zeros((ny, LANES), F32)

    def absorb(c, holes, k):
        for t in range(wide // LANES):
            if c == 1 and t % (part // LANES) == 0:
                hole_copy(2 * k + t // (part // LANES)).wait_recv()
            real, imag = products(holes, k * (wide // LANES) + t)
            moved_real = pltpu.roll(real, LANES // 2, 1)
            moved_imag = pltpu.roll(imag, LANES // 2, 1)
            stage_ref[pl.ds(2 * t, rows, stride=CHUNK), :] = jnp.where(
                first_half, real, moved_imag
            )
            stage_ref[pl.ds(2 * t + 1, rows, stride=CHUNK), :] = jnp.where(
                first_half, moved_real, imag
            )
        high, low = split(stage_ref[...])
        both = jnp.dot(
            jnp.concatenate([high, low], 1), zf_ref[...], preferred_element_type=F32
        )
        deep = both[:, :LANES] + both[:, LANES:]
        turn = turned(deep, sign)
        table = chunk_ref[k][:, : 6 * CHUNK]
        for x in range(0, rows, 2):
            pair = []
            for j in (x, x + 1):
                own = slice(j * CHUNK, (j + 1) * CHUNK)
                pair.append(jnp.concatenate([deep[own], turn[own]], 0))
            high, low = split(jnp.concatenate(pair, 1))
            share = jnp.dot(
                table, jnp.concatenate([high, low, high], 0), preferred_element_type=F32
            )
            for j in range(2):
                own = slice((x + j) * ny, (x + j + 1) * ny)
                rho_ref[c, own, :] = rho_ref[c, own, :] + share[:, j * LANES : (j + 1) * LANES]

    planes = min(rows, 4)
    span = planes * ny
    block = 16

    fields = [fld_ref, out_ref]

    empty = jnp.zeros((block, LANES), F32)
    zero_row = jnp.zeros((1, LANES), F32)

    def sweep(c):
        def body(i, sums):
            energy, cross_real, cross_imag = sums
            at = pl.multiple_of(i * block, block)
            decay = tab_ref[0, pl.ds(at, block), :]
            response = tab_ref[1, pl.ds(at, block), :]
            left = right = empty
            spread = []
            for x in reversed(range(rows)):
                right = decay * right
                spread.append(right)
                right = right + rho_ref[c, pl.ds(x * ny + at, block), :]
            for x in range(rows):
                own = pl.ds(x * ny + at, block)
                value = rho_ref[c, own, :]
                left = decay * left + value
                field = response * (left + spread[rows - 1 - x])
                fields[c][own, :] = field
                energy = energy + field * value
                if c == 1:
                    cross_real = cross_real + fld_ref[own, :] * value
                    cross_imag = cross_imag + turn_ref[own, :] * value
            msg_ref[c, pl.ds(at, block), :] = left
            msg_ref[c, pl.ds(ny + at, block), :] = right
            return energy, cross_real, cross_imag

        sums = lax.fori_loop(0, ny // block, body, (empty,) * 3, unroll=2)
        total = rho_ref[c, 0:8, :]
        for x in range(1, rows):
            total = total + rho_ref[c, x * ny : x * ny + 8, :]
        tail = [total[0:1]] + [jnp.sum(part, axis=0, keepdims=True) for part in sums]
        msg_ref[c, 2 * ny : 2 * ny + 8, :] = jnp.concatenate(tail + [zero_row] * 4, 0)
        copies = []
        for j in range(n - 1):
            slot = lax.rem(others[j] - me - 1 + n, n)
            copies.append(
                pltpu.make_async_remote_copy(
                    src_ref=msg_ref.at[c], dst_ref=recv_ref.at[c, slot],
                    send_sem=msg_send.at[c, j], recv_sem=msg_recv.at[c, slot],
                    device_id=(group, others[j]), device_id_type=MESH,
                )
            )
        for copy in copies:
            copy.start()
        return copies

    def arrive(c):
        for k in range(n - 1):
            pltpu.make_async_remote_copy(
                src_ref=msg_ref.at[c], dst_ref=recv_ref.at[c, k],
                send_sem=msg_send.at[c, k], recv_sem=msg_recv.at[c, k],
                device_id=(group, others[k]), device_id_type=MESH,
            ).wait_recv()

    def tails(c, row):
        total = msg_ref[c, 2 * ny + row : 2 * ny + row + 1, :]
        for k in range(n - 1):
            total = total + recv_ref[c, k, 2 * ny + row : 2 * ny + row + 1, :]
        return total

    def solve(c):
        mean = tails(c, 0)

        def body(i, energy):
            at = pl.multiple_of(i * block, block)
            decay = tab_ref[0, pl.ds(at, block), :]
            response = tab_ref[1, pl.ds(at, block), :]
            background = tab_ref[2, pl.ds(at, block), :] * mean
            weights = [tab_ref[3 + k, pl.ds(at, block), :] for k in range(n)]
            rights = [msg_ref[c, pl.ds(at, block), :]]
            lefts = [msg_ref[c, pl.ds(ny + at, block), :]]
            for k in range(n - 1):
                rights.append(recv_ref[c, k, pl.ds(at, block), :])
                lefts.append(recv_ref[c, k, pl.ds(ny + at, block), :])
            left = right = pairs = empty
            for a in range(n):
                coming = empty
                for k in range(n):
                    coming = coming + weights[k] * rights[(a + k + 1) % n]
                pairs = pairs + coming * lefts[a]
                if a == 0:
                    left = coming
            for k in range(n):
                right = right + weights[k] * lefts[(n - k - 1) % n]
            energy = energy + 2.0 * response * decay * pairs - background * mean
            left = response * left
            right = response * right
            spread = []
            for x in range(rows):
                right = decay * right
                spread.append(right)
            for x in range(rows):
                left = decay * left
                own = pl.ds(x * ny + at, block)
                fields[c][own, :] = fields[c][own, :] + (
                    left + spread[rows - 1 - x] - background
                )
            return energy

        total = lax.fori_loop(0, ny // block, body, empty)
        return jnp.sum(total, axis=0, keepdims=True)

    for copy in loads:
        copy.wait()

    clear(0)
    clear(1)

    @pl.loop(0, chunks)
    def _(k):
        absorb(0, h_ref, k)

    @pl.when(jnp.logical_not(even))
    def _():
        pl.semaphore_wait(ready_sem, 1)

    copies0 = sweep(0)

    early = min(chunks, 2)

    @pl.loop(0, early)
    def _(k):
        absorb(1, prev_ref, k)

    arrive(0)
    sum_ref[0:1, :] = tails(0, 1) + solve(0)

    @pl.loop(0, rows // planes)
    def _(i):
        own = pl.ds(pl.multiple_of(i * span, span), span)
        values = fld_ref[own, :]
        turn_ref[own, :] = turned(values, sign)
        res_ref[own, :] = inverse(values, zi_ref, yi_ref, ny, sign)

    @pl.loop(early, chunks)
    def _(k):
        absorb(1, prev_ref, k)

    copies1 = sweep(1)
    arrive(1)
    sum_ref[1:2, :] = tails(1, 1) + solve(1)
    sum_ref[2:3, :] = tails(1, 2)
    sum_ref[3:4, :] = tails(1, 3)
    sum_ref[4:8, :] = jnp.zeros((4, LANES), F32)

    for copy in [hole_copy(k) for k in range(2 * chunks)] + copies0 + copies1:
        copy.wait_send()


def finish(
    ny, scale, order_ref, res_ref, fld_ref, sum_ref, back_ref, out_ref, coul_ref
):
    flat = res_ref.shape[0]
    first, second = order_ref[0:1, 0:1], order_ref[0:1, 1:2]
    sign = sign_of(lax.broadcasted_iota(jnp.int32, (1, LANES), 1))
    span = min(flat // ny, 4) * ny
    for i in range(flat // span):
        own = slice(i * span, (i + 1) * span)
        values = inverse(
            fld_ref[own, :], back_ref.at[0 : 2 * LANES], back_ref.at[2 * LANES : 3 * LANES],
            ny, sign,
        )
        stored = res_ref[own, :]
        out_ref[0, own, :] = jnp.where(first == 0, stored, values)
        out_ref[1, own, :] = jnp.where(second == 0, stored, values)

    entries = [jnp.sum(sum_ref[k : k + 1, :]) * scale for k in range(4)]
    shape = (2, 2, 2)
    part_of = lax.broadcasted_iota(jnp.int32, shape, 0)
    row = lax.broadcasted_iota(jnp.int32, shape, 1)
    column = lax.broadcasted_iota(jnp.int32, shape, 2)
    row_pair = jnp.where(row == 0, first[None], second[None])
    column_pair = jnp.where(column == 0, first[None], second[None])
    same = row_pair == column_pair
    opening = row_pair == 0
    real = jnp.where(same, jnp.where(opening, entries[0], entries[1]), entries[2])
    imag = jnp.where(same, 0.0, jnp.where(opening, entries[3], -entries[3]))
    coul_ref[0] = jnp.where(part_of == 0, real, imag)


def shards(n, blocks, electrons, holes, pair_order):
    _, bands, parts, rows, cells = electrons.shape
    ny = nz = math.isqrt(cells)
    flat = rows * ny
    nx = rows * n
    vmem = pl.BlockSpec(memory_space=pltpu.VMEM)
    hbm = pl.BlockSpec(memory_space=pl.ANY)
    states = (bands, parts, rows, cells)
    message = 2 * ny + 8
    chunks = ny // CHUNK
    back = np.concatenate([depth_table(nz, -1.0), column_table(ny, -1.0)])
    tables = solver_tables(nx, ny, nz, n)
    stored, field, sums, back_kept = pl.pallas_call(
        functools.partial(kernel, n, blocks, ny),
        out_shape=(
            pltpu.VMEM((flat, LANES), F32),
            pltpu.VMEM((flat, LANES), F32),
            pltpu.VMEM((8, LANES), F32),
            pltpu.VMEM(back.shape, BF16),
        ),
        in_specs=[hbm] * 6,
        out_specs=(vmem,) * 4,
        scratch_shapes=[
            pltpu.VMEM(states, BF16),
            pltpu.VMEM(states, BF16),
            pltpu.VMEM(states, BF16),
            pltpu.VMEM((rows * CHUNK, LANES), F32),
            pltpu.VMEM((2, flat, LANES), F32),
            pltpu.VMEM((flat, LANES), F32),
            pltpu.VMEM((2, message, LANES), F32),
            pltpu.VMEM((2, n - 1, message, LANES), F32),
            pltpu.VMEM((flat, LANES), F32),
            pltpu.VMEM((2 * LANES, 2 * LANES), BF16),
            pltpu.VMEM((chunks, ny, LANES), BF16),
            pltpu.VMEM(tables.shape, F32),
            pltpu.SemaphoreType.DMA((6,)),
            pltpu.SemaphoreType.DMA((2 * chunks,)),
            pltpu.SemaphoreType.DMA((2 * chunks,)),
            pltpu.SemaphoreType.DMA((2, n - 1)),
            pltpu.SemaphoreType.DMA((2, n - 1)),
            pltpu.SemaphoreType.REGULAR,
            pltpu.SemaphoreType.REGULAR,
        ],
        compiler_params=pltpu.CompilerParams(
            collective_id=0, has_side_effects=True, vmem_limit_bytes=60 * 2**20
        ),
        name="screened",
    )(
        electrons,
        holes,
        jnp.asarray(depth_table(nz, 1.0)),
        jnp.asarray(chunk_table(ny)),
        jnp.asarray(back),
        jnp.asarray(tables),
    )
    potential, coulomb = pl.pallas_call(
        functools.partial(finish, ny, 1.0 / (nx * cells)),
        out_shape=(
            jax.ShapeDtypeStruct((2, flat, LANES), F32),
            jax.ShapeDtypeStruct((1, 2, 2, 2), F32),
        ),
        in_specs=[vmem] * 5,
        out_specs=(vmem, vmem),
        compiler_params=pltpu.CompilerParams(vmem_limit_bytes=16 * 2**20),
        name="finish",
    )(pair_order, stored, field, sums, back_kept)
    return potential.reshape(1, 2, rows, ny, 2 * nz), coulomb


def solution(mesh):
    body = functools.partial(shards, mesh.shape["space"], mesh.shape["blk"])
    in_specs = (
        P("blk", None, None, "space", None),
        P("blk", None, None, "space", None),
        P("blk", None),
    )
    out_specs = (P("blk", None, "space", None, None), P("blk", None, None, None))
    return jax.shard_map(body, mesh=mesh, in_specs=in_specs, out_specs=out_specs, check_vma=False)
```

```python
import functools
import math

import jax
import jax.numpy as jnp
import numpy as np
from jax import lax
from jax.experimental import pallas as pl
from jax.experimental.pallas import tpu as pltpu
from jax.sharding import PartitionSpec as P

SCREENING = 0.01
MESH = pl.DeviceIdType.MESH
LANES = 128
CHUNK = 8
F32 = jnp.float32
BF16 = jnp.bfloat16


def halves(matrix):
    high = matrix.astype(jnp.bfloat16)
    low = (matrix - high.astype(np.float64)).astype(jnp.bfloat16)
    return high, low


def phases(points):
    positions = np.arange(points)
    angles = 2.0 * math.pi / points * (np.outer(positions, positions) % points)
    return np.cos(angles), np.sin(angles)


def depth_table(points, direction):
    cosines, sines = phases(points)
    sines = direction * sines
    matrix = np.concatenate(
        [np.concatenate([cosines, -sines], 1), np.concatenate([sines, cosines], 1)], 0
    )
    high, low = halves(matrix)
    top = np.concatenate([high, low], 1)
    bottom = np.concatenate([high, np.zeros_like(high)], 1)
    return np.concatenate([top, bottom], 0)


def column_table(points, direction):
    cosines, sines = phases(points)
    high, low = halves(np.concatenate([cosines, direction * sines], 1))
    top = np.concatenate([high, high], 1)
    bottom = np.concatenate([low, np.zeros_like(low)], 1)
    return np.concatenate([top, bottom], 0)


def chunk_table(points):
    cosines, sines = phases(points)
    tables = []
    for start in range(0, points, CHUNK):
        own = slice(start, start + CHUNK)
        high, low = halves(np.concatenate([cosines[:, own], sines[:, own]], 1))
        fill = np.zeros((points, LANES - 6 * CHUNK), high.dtype)
        tables.append(np.concatenate([high, high, low, fill], 1))
    return np.stack(tables)


def solver_tables(nx, ny, nz, devices):
    term_y = 2.0 - 2.0 * np.cos(2.0 * math.pi / ny * np.arange(ny))
    term_z = 2.0 - 2.0 * np.cos(2.0 * math.pi / nz * (np.arange(2 * nz) % nz))
    shift = term_y[:, None] + term_z[None, :] + SCREENING
    root = np.sqrt(shift * (shift + 4.0))
    decay = 2.0 / (shift + 2.0 + root)
    response = 1.0 / root / (ny * nz)
    anchor = np.zeros_like(shift)
    anchor[0, 0] = anchor[0, nz] = 1.0 / (SCREENING * nx * ny * nz)
    rows = nx // devices
    weights = [decay ** (rows * j) / (1.0 - decay**nx) for j in range(devices)]
    return np.stack([decay, response, anchor] + weights).astype(np.float32)


def split(values):
    high = values.astype(BF16)
    return high, (values - high.astype(F32)).astype(BF16)


def turned(values, sign):
    return pltpu.roll(values, LANES // 2, values.ndim - 1) * sign


def sign_of(lane):
    return jnp.where(lane < LANES // 2, 1.0, -1.0).astype(F32)


def inverse(values, z_ref, y_ref, ny, sign):
    planes = values.shape[0] // ny
    high, low = split(values)
    wide = jnp.dot(jnp.concatenate([high, low], 1), z_ref[...], preferred_element_type=F32)
    deep = wide[:, :LANES] + wide[:, LANES:]
    turn = turned(deep, sign)
    high, low = split(deep)
    turn_high, turn_low = split(turn)
    parts = []
    for x in range(0, planes, 2):
        columns = []
        for k in (x, x + 1):
            own = slice(k * ny, (k + 1) * ny)
            columns.append(
                jnp.concatenate([high[own], turn_high[own], low[own], turn_low[own]], 0)
            )
        both = jnp.dot(y_ref[...], jnp.concatenate(columns, 1), preferred_element_type=F32)
        total = both[:ny] + both[ny:]
        parts += [total[:, :LANES], total[:, LANES:]]
    return jnp.concatenate(parts, 0)


def kernel(
    n, blocks, ny,
    e_hbm, h_hbm, zf_hbm, chunk_hbm, back_hbm, tab_hbm,
    res_ref, out_ref, sum_ref, back_ref,
    e_ref, h_ref, prev_ref, stage_ref, rho_ref, fld_ref, msg_ref, recv_ref,
    turn_ref, relay_ref, zf_ref, chunk_ref, tab_ref,
    load_sem, hole_send, hole_recv, msg_send, msg_recv, relay_send, relay_recv, greet_sem, ready_sem,
):
    bands, _, rows, cells = e_ref.shape
    chunks = ny // CHUNK
    wide = cells // chunks
    group = lax.axis_index("blk")
    me = lax.axis_index("space")
    following = lax.rem(group + 1, blocks)
    preceding = lax.rem(group + blocks - 1, blocks)
    others = [j + (me <= j).astype(jnp.int32) for j in range(n - 1)]

    loads = [
        pltpu.make_async_copy(e_hbm.at[0], e_ref, load_sem.at[0]),
        pltpu.make_async_copy(h_hbm.at[0], h_ref, load_sem.at[1]),
        pltpu.make_async_copy(zf_hbm, zf_ref, load_sem.at[2]),
        pltpu.make_async_copy(chunk_hbm, chunk_ref, load_sem.at[3]),
        pltpu.make_async_copy(back_hbm, back_ref, load_sem.at[4]),
        pltpu.make_async_copy(tab_hbm, tab_ref, load_sem.at[5]),
    ]
    zi_ref = back_ref.at[0 : 2 * LANES]
    yi_ref = back_ref.at[2 * LANES : 3 * LANES]
    last = 2 * chunks - 2
    part = wide // 2
    pieces = [slice(last * part, last * part + part // 2), slice(last * part + part // 2, (last + 1) * part)]
    entries = [last, 2 * chunks]
    source, relay = blocks - 1, 2
    relayed = blocks > 4
    detour = group == (source if relayed else -1)
    onward = group == (relay if relayed else -1)

    def hole_copy(k):
        window = pl.ds(pl.multiple_of(k * part, part), part)
        return pltpu.make_async_remote_copy(
            src_ref=h_hbm.at[0, :, :, :, window], dst_ref=prev_ref.at[:, :, :, window],
            send_sem=hole_send.at[k], recv_sem=hole_recv.at[k],
            device_id=(following, me), device_id_type=MESH,
        )

    def piece_copy(i):
        return pltpu.make_async_remote_copy(
            src_ref=h_hbm.at[0, :, :, :, pieces[i]], dst_ref=prev_ref.at[:, :, :, pieces[i]],
            send_sem=hole_send.at[entries[i]], recv_sem=hole_recv.at[entries[i]],
            device_id=(following, me), device_id_type=MESH,
        )

    def detour_copy():
        return pltpu.make_async_remote_copy(
            src_ref=h_hbm.at[0, :, :, :, pieces[0]], dst_ref=relay_ref,
            send_sem=hole_send.at[entries[0]], recv_sem=relay_recv,
            device_id=(relay, me), device_id_type=MESH,
        )

    def onward_copy():
        return pltpu.make_async_remote_copy(
            src_ref=relay_ref, dst_ref=prev_ref.at[:, :, :, pieces[0]],
            send_sem=relay_send, recv_sem=hole_recv.at[entries[0]],
            device_id=(0, me), device_id_type=MESH,
        )

    def start_holes():
        for k in range(last):
            hole_copy(k).start()
        pl.when(jnp.logical_not(detour))(piece_copy(0).start)
        piece_copy(1).start()
        hole_copy(last + 1).start()

    even = lax.rem(group, 2) == 0
    barrier = pltpu.get_barrier_semaphore()
    pl.semaphore_signal(barrier, inc=1, device_id=(preceding, me), device_id_type=MESH)

    if relayed:
        @pl.when(onward)
        def _():
            pl.semaphore_signal(barrier, inc=1, device_id=(source, me), device_id_type=MESH)

    @pl.when(even)
    def _():
        for other in others:
            pl.semaphore_signal(barrier, inc=1, device_id=(group, other), device_id_type=MESH)

    for copy in loads:
        copy.start()

    @pl.when(jnp.logical_not(even))
    def _():
        pl.semaphore_wait(barrier, jnp.where(detour, 2, 1))
        pl.when(detour)(detour_copy().start)
        start_holes()

    @pl.when(even)
    def _():
        pl.semaphore_wait(barrier, n)
        start_holes()
        for other in others:
            pl.semaphore_signal(greet_sem, inc=1, device_id=(group, other), device_id_type=MESH)
        pl.semaphore_wait(greet_sem, n - 1)
        pl.semaphore_signal(ready_sem, inc=1, device_id=(following, me), device_id_type=MESH)

    lane = lax.broadcasted_iota(jnp.int32, (1, LANES), 1)
    first_half = lane < LANES // 2
    sign = sign_of(lane)

    def products(holes, t):
        window = pl.ds(pl.multiple_of(t * LANES, LANES), LANES)
        real = imag = None
        for b in range(bands):
            er = e_ref[b, 0, :, window].astype(F32)
            ei = e_ref[b, 1, :, window].astype(F32)
            hr = holes[b, 0, :, window].astype(F32)
            hi = holes[b, 1, :, window].astype(F32)
            if b == 0:
                real, imag = er * hr + ei * hi, er * hi - ei * hr
            else:
                real = real + (er * hr + ei * hi)
                imag = imag + (er * hi - ei * hr)
        return real, imag

    def clear(c):
        @pl.loop(0, rows)
        def _(x):
            rho_ref[c, pl.ds(pl.multiple_of(x * ny, ny), ny), :] = jnp.zeros((ny, LANES), F32)

    def absorb(c, holes, k, waits=None):
        for t in range(wide // LANES):
            if c == 1 and t % (part // LANES) == 0:
                if waits is None:
                    hole_copy(2 * k + t // (part // LANES)).wait_recv()
                else:
                    waits[t // (part // LANES)]()
            real, imag = products(holes, k * (wide // LANES) + t)
            moved_real = pltpu.roll(real, LANES // 2, 1)
            moved_imag = pltpu.roll(imag, LANES // 2, 1)
            stage_ref[pl.ds(2 * t, rows, stride=CHUNK), :] = jnp.where(
                first_half, real, moved_imag
            )
            stage_ref[pl.ds(2 * t + 1, rows, stride=CHUNK), :] = jnp.where(
                first_half, moved_real, imag
            )
        high, low = split(stage_ref[...])
        both = jnp.dot(
            jnp.concatenate([high, low], 1), zf_ref[...], preferred_element_type=F32
        )
        deep = both[:, :LANES] + both[:, LANES:]
        turn = turned(deep, sign)
        table = chunk_ref[k][:, : 6 * CHUNK]
        for x in range(0, rows, 2):
            pair = []
            for j in (x, x + 1):
                own = slice(j * CHUNK, (j + 1) * CHUNK)
                pair.append(jnp.concatenate([deep[own], turn[own]], 0))
            high, low = split(jnp.concatenate(pair, 1))
            share = jnp.dot(
                table, jnp.concatenate([high, low, high], 0), preferred_element_type=F32
            )
            for j in range(2):
                own = slice((x + j) * ny, (x + j + 1) * ny)
                rho_ref[c, own, :] = rho_ref[c, own, :] + share[:, j * LANES : (j + 1) * LANES]

    planes = min(rows, 4)
    span = planes * ny
    block = 16

    fields = [fld_ref, out_ref]

    empty = jnp.zeros((block, LANES), F32)
    zero_row = jnp.zeros((1, LANES), F32)

    def sweep(c):
        def body(i, sums):
            energy, cross_real, cross_imag = sums
            at = pl.multiple_of(i * block, block)
            decay = tab_ref[0, pl.ds(at, block), :]
            response = tab_ref[1, pl.ds(at, block), :]
            left = right = empty
            spread = []
            for x in reversed(range(rows)):
                right = decay * right
                spread.append(right)
                right = right + rho_ref[c, pl.ds(x * ny + at, block), :]
            for x in range(rows):
                own = pl.ds(x * ny + at, block)
                value = rho_ref[c, own, :]
                left = decay * left + value
                field = response * (left + spread[rows - 1 - x])
                fields[c][own, :] = field
                energy = energy + field * value
                if c == 1:
                    cross_real = cross_real + fld_ref[own, :] * value
                    cross_imag = cross_imag + turn_ref[own, :] * value
            msg_ref[c, pl.ds(at, block), :] = left
            msg_ref[c, pl.ds(ny + at, block), :] = right
            return energy, cross_real, cross_imag

        sums = lax.fori_loop(0, ny // block, body, (empty,) * 3, unroll=2)
        total = rho_ref[c, 0:8, :]
        for x in range(1, rows):
            total = total + rho_ref[c, x * ny : x * ny + 8, :]
        tail = [total[0:1]] + [jnp.sum(part, axis=0, keepdims=True) for part in sums]
        msg_ref[c, 2 * ny : 2 * ny + 8, :] = jnp.concatenate(tail + [zero_row] * 4, 0)
        copies = []
        for j in range(n - 1):
            slot = lax.rem(others[j] - me - 1 + n, n)
            copies.append(
                pltpu.make_async_remote_copy(
                    src_ref=msg_ref.at[c], dst_ref=recv_ref.at[c, slot],
                    send_sem=msg_send.at[c, j], recv_sem=msg_recv.at[c, slot],
                    device_id=(group, others[j]), device_id_type=MESH,
                )
            )
        for copy in copies:
            copy.start()
        return copies

    def arrive(c):
        for k in range(n - 1):
            pltpu.make_async_remote_copy(
                src_ref=msg_ref.at[c], dst_ref=recv_ref.at[c, k],
                send_sem=msg_send.at[c, k], recv_sem=msg_recv.at[c, k],
                device_id=(group, others[k]), device_id_type=MESH,
            ).wait_recv()

    def tails(c, row):
        total = msg_ref[c, 2 * ny + row : 2 * ny + row + 1, :]
        for k in range(n - 1):
            total = total + recv_ref[c, k, 2 * ny + row : 2 * ny + row + 1, :]
        return total

    def solve(c):
        mean = tails(c, 0)

        def body(i, energy):
            at = pl.multiple_of(i * block, block)
            decay = tab_ref[0, pl.ds(at, block), :]
            response = tab_ref[1, pl.ds(at, block), :]
            background = tab_ref[2, pl.ds(at, block), :] * mean
            weights = [tab_ref[3 + k, pl.ds(at, block), :] for k in range(n)]
            rights = [msg_ref[c, pl.ds(at, block), :]]
            lefts = [msg_ref[c, pl.ds(ny + at, block), :]]
            for k in range(n - 1):
                rights.append(recv_ref[c, k, pl.ds(at, block), :])
                lefts.append(recv_ref[c, k, pl.ds(ny + at, block), :])
            left = right = pairs = empty
            for a in range(n):
                coming = empty
                for k in range(n):
                    coming = coming + weights[k] * rights[(a + k + 1) % n]
                pairs = pairs + coming * lefts[a]
                if a == 0:
                    left = coming
            for k in range(n):
                right = right + weights[k] * lefts[(n - k - 1) % n]
            energy = energy + 2.0 * response * decay * pairs - background * mean
            left = response * left
            right = response * right
            spread = []
            for x in range(rows):
                right = decay * right
                spread.append(right)
            for x in range(rows):
                left = decay * left
                own = pl.ds(x * ny + at, block)
                fields[c][own, :] = fields[c][own, :] + (
                    left + spread[rows - 1 - x] - background
                )
            return energy

        total = lax.fori_loop(0, ny // block, body, empty)
        return jnp.sum(total, axis=0, keepdims=True)

    for copy in loads:
        copy.wait()

    clear(0)
    clear(1)

    @pl.loop(0, chunks)
    def _(k):
        absorb(0, h_ref, k)

    @pl.when(jnp.logical_not(even))
    def _():
        pl.semaphore_wait(ready_sem, 1)

    copies0 = sweep(0)

    early = min(chunks, 2)

    @pl.loop(0, early)
    def _(k):
        absorb(1, prev_ref, k)

    arrive(0)
    sum_ref[0:1, :] = tails(0, 1) + solve(0)

    @pl.loop(0, rows // planes)
    def _(i):
        own = pl.ds(pl.multiple_of(i * span, span), span)
        values = fld_ref[own, :]
        turn_ref[own, :] = turned(values, sign)
        res_ref[own, :] = inverse(values, zi_ref, yi_ref, ny, sign)

    if relayed:
        @pl.when(onward)
        def _():
            detour_copy().wait_recv()
            onward_copy().start()

    @pl.loop(early, chunks - 1)
    def _(k):
        absorb(1, prev_ref, k)

    def split_wait():
        for i in range(2):
            piece_copy(i).wait_recv()

    absorb(1, prev_ref, chunks - 1, [split_wait, hole_copy(last + 1).wait_recv])

    copies1 = sweep(1)
    for k in range(last):
        hole_copy(k).wait_send()
    for copy in [hole_copy(last + 1)] + [piece_copy(i) for i in range(2)] + copies0:
        copy.wait_send()
    if relayed:
        pl.when(onward)(onward_copy().wait_send)
    arrive(1)
    sum_ref[1:2, :] = tails(1, 1) + solve(1)
    sum_ref[2:3, :] = tails(1, 2)
    sum_ref[3:4, :] = tails(1, 3)
    sum_ref[4:8, :] = jnp.zeros((4, LANES), F32)

    for copy in copies1:
        copy.wait_send()


def finish(
    ny, scale, order_ref, res_ref, fld_ref, sum_ref, back_ref, out_ref, coul_ref
):
    flat = res_ref.shape[0]
    first, second = order_ref[0:1, 0:1], order_ref[0:1, 1:2]
    sign = sign_of(lax.broadcasted_iota(jnp.int32, (1, LANES), 1))
    span = min(flat // ny, 4) * ny
    for i in range(flat // span):
        own = slice(i * span, (i + 1) * span)
        values = inverse(
            fld_ref[own, :], back_ref.at[0 : 2 * LANES], back_ref.at[2 * LANES : 3 * LANES],
            ny, sign,
        )
        stored = res_ref[own, :]
        out_ref[0, own, :] = jnp.where(first == 0, stored, values)
        out_ref[1, own, :] = jnp.where(second == 0, stored, values)

    entries = [jnp.sum(sum_ref[k : k + 1, :]) * scale for k in range(4)]
    shape = (2, 2, 2)
    part_of = lax.broadcasted_iota(jnp.int32, shape, 0)
    row = lax.broadcasted_iota(jnp.int32, shape, 1)
    column = lax.broadcasted_iota(jnp.int32, shape, 2)
    row_pair = jnp.where(row == 0, first[None], second[None])
    column_pair = jnp.where(column == 0, first[None], second[None])
    same = row_pair == column_pair
    opening = row_pair == 0
    real = jnp.where(same, jnp.where(opening, entries[0], entries[1]), entries[2])
    imag = jnp.where(same, 0.0, jnp.where(opening, entries[3], -entries[3]))
    coul_ref[0] = jnp.where(part_of == 0, real, imag)


def shards(n, blocks, electrons, holes, pair_order):
    _, bands, parts, rows, cells = electrons.shape
    ny = nz = math.isqrt(cells)
    flat = rows * ny
    nx = rows * n
    vmem = pl.BlockSpec(memory_space=pltpu.VMEM)
    hbm = pl.BlockSpec(memory_space=pl.ANY)
    states = (bands, parts, rows, cells)
    message = 2 * ny + 8
    chunks = ny // CHUNK
    back = np.concatenate([depth_table(nz, -1.0), column_table(ny, -1.0)])
    tables = solver_tables(nx, ny, nz, n)
    stored, field, sums, back_kept = pl.pallas_call(
        functools.partial(kernel, n, blocks, ny),
        out_shape=(
            pltpu.VMEM((flat, LANES), F32),
            pltpu.VMEM((flat, LANES), F32),
            pltpu.VMEM((8, LANES), F32),
            pltpu.VMEM(back.shape, BF16),
        ),
        in_specs=[hbm] * 6,
        out_specs=(vmem,) * 4,
        scratch_shapes=[
            pltpu.VMEM(states, BF16),
            pltpu.VMEM(states, BF16),
            pltpu.VMEM(states, BF16),
            pltpu.VMEM((rows * CHUNK, LANES), F32),
            pltpu.VMEM((2, flat, LANES), F32),
            pltpu.VMEM((flat, LANES), F32),
            pltpu.VMEM((2, message, LANES), F32),
            pltpu.VMEM((2, n - 1, message, LANES), F32),
            pltpu.VMEM((flat, LANES), F32),
            pltpu.VMEM((bands, parts, rows, cells // chunks // 4), BF16),
            pltpu.VMEM((2 * LANES, 2 * LANES), BF16),
            pltpu.VMEM((chunks, ny, LANES), BF16),
            pltpu.VMEM(tables.shape, F32),
            pltpu.SemaphoreType.DMA((6,)),
            pltpu.SemaphoreType.DMA((2 * chunks + 1,)),
            pltpu.SemaphoreType.DMA((2 * chunks + 1,)),
            pltpu.SemaphoreType.DMA((2, n - 1)),
            pltpu.SemaphoreType.DMA((2, n - 1)),
            pltpu.SemaphoreType.DMA,
            pltpu.SemaphoreType.DMA,
            pltpu.SemaphoreType.REGULAR,
            pltpu.SemaphoreType.REGULAR,
        ],
        compiler_params=pltpu.CompilerParams(
            collective_id=0, has_side_effects=True, vmem_limit_bytes=60 * 2**20
        ),
        name="screened",
    )(
        electrons,
        holes,
        jnp.asarray(depth_table(nz, 1.0)),
        jnp.asarray(chunk_table(ny)),
        jnp.asarray(back),
        jnp.asarray(tables),
    )
    potential, coulomb = pl.pallas_call(
        functools.partial(finish, ny, 1.0 / (nx * cells)),
        out_shape=(
            jax.ShapeDtypeStruct((2, flat, LANES), F32),
            jax.ShapeDtypeStruct((1, 2, 2, 2), F32),
        ),
        in_specs=[vmem] * 5,
        out_specs=(vmem, vmem),
        compiler_params=pltpu.CompilerParams(vmem_limit_bytes=16 * 2**20),
        name="finish",
    )(pair_order, stored, field, sums, back_kept)
    return potential.reshape(1, 2, rows, ny, 2 * nz), coulomb


def solution(mesh):
    body = functools.partial(shards, mesh.shape["space"], mesh.shape["blk"])
    in_specs = (
        P("blk", None, None, "space", None),
        P("blk", None, None, "space", None),
        P("blk", None),
    )
    out_specs = (P("blk", None, "space", None, None), P("blk", None, None, None))
    return jax.shard_map(body, mesh=mesh, in_specs=in_specs, out_specs=out_specs, check_vma=False)
```

```python
import functools
import math

import jax
import jax.numpy as jnp
import numpy as np
from jax import lax
from jax.experimental import pallas as pl
from jax.experimental.pallas import tpu as pltpu
from jax.sharding import PartitionSpec as P

SCREENING = 0.01
MESH = pl.DeviceIdType.MESH
LANES = 128
CHUNK = 8
F32 = jnp.float32
BF16 = jnp.bfloat16


def halves(matrix):
    high = matrix.astype(jnp.bfloat16)
    low = (matrix - high.astype(np.float64)).astype(jnp.bfloat16)
    return high, low


def phases(points):
    positions = np.arange(points)
    angles = 2.0 * math.pi / points * (np.outer(positions, positions) % points)
    return np.cos(angles), np.sin(angles)


def depth_table(points, direction):
    cosines, sines = phases(points)
    sines = direction * sines
    matrix = np.concatenate(
        [np.concatenate([cosines, -sines], 1), np.concatenate([sines, cosines], 1)], 0
    )
    high, low = halves(matrix)
    top = np.concatenate([high, low], 1)
    bottom = np.concatenate([high, np.zeros_like(high)], 1)
    return np.concatenate([top, bottom], 0)


def column_table(points, direction):
    cosines, sines = phases(points)
    high, low = halves(np.concatenate([cosines, direction * sines], 1))
    top = np.concatenate([high, high], 1)
    bottom = np.concatenate([low, np.zeros_like(low)], 1)
    return np.concatenate([top, bottom], 0)


def chunk_table(points):
    cosines, sines = phases(points)
    tables = []
    for start in range(0, points, CHUNK):
        own = slice(start, start + CHUNK)
        high, low = halves(np.concatenate([cosines[:, own], sines[:, own]], 1))
        fill = np.zeros((points, LANES - 6 * CHUNK), high.dtype)
        tables.append(np.concatenate([high, high, low, fill], 1))
    return np.stack(tables)


def solver_tables(nx, ny, nz, devices):
    term_y = 2.0 - 2.0 * np.cos(2.0 * math.pi / ny * np.arange(ny))
    term_z = 2.0 - 2.0 * np.cos(2.0 * math.pi / nz * (np.arange(2 * nz) % nz))
    shift = term_y[:, None] + term_z[None, :] + SCREENING
    root = np.sqrt(shift * (shift + 4.0))
    decay = 2.0 / (shift + 2.0 + root)
    response = 1.0 / root / (ny * nz)
    anchor = np.zeros_like(shift)
    anchor[0, 0] = anchor[0, nz] = 1.0 / (SCREENING * nx * ny * nz)
    rows = nx // devices
    weights = [decay ** (rows * j) / (1.0 - decay**nx) for j in range(devices)]
    return np.stack([decay, response, anchor] + weights).astype(np.float32)


def split(values):
    high = values.astype(BF16)
    return high, (values - high.astype(F32)).astype(BF16)


def turned(values, sign):
    return pltpu.roll(values, LANES // 2, values.ndim - 1) * sign


def sign_of(lane):
    return jnp.where(lane < LANES // 2, 1.0, -1.0).astype(F32)


def inverse(values, z_ref, y_ref, ny, sign):
    planes = values.shape[0] // ny
    high, low = split(values)
    wide = jnp.dot(jnp.concatenate([high, low], 1), z_ref[...], preferred_element_type=F32)
    deep = wide[:, :LANES] + wide[:, LANES:]
    turn = turned(deep, sign)
    high, low = split(deep)
    turn_high, turn_low = split(turn)
    parts = []
    for x in range(0, planes, 2):
        columns = []
        for k in (x, x + 1):
            own = slice(k * ny, (k + 1) * ny)
            columns.append(
                jnp.concatenate([high[own], turn_high[own], low[own], turn_low[own]], 0)
            )
        both = jnp.dot(y_ref[...], jnp.concatenate(columns, 1), preferred_element_type=F32)
        total = both[:ny] + both[ny:]
        parts += [total[:, :LANES], total[:, LANES:]]
    return jnp.concatenate(parts, 0)


def kernel(
    n, blocks, ny,
    e_hbm, h_hbm, zf_hbm, chunk_hbm, back_hbm, tab_hbm,
    res_ref, out_ref, sum_ref, back_ref,
    e_ref, h_ref, prev_ref, stage_ref, rho_ref, fld_ref, msg_ref, recv_ref,
    turn_ref, relay_ref, visit_ref, answer_ref, reply_ref, zf_ref, chunk_ref, tab_ref,
    load_sem, hole_send, hole_recv, msg_send, msg_recv, relay_send, relay_recv, swap_send, swap_recv, greet_sem, ready_sem,
):
    bands, _, rows, cells = e_ref.shape
    chunks = ny // CHUNK
    wide = cells // chunks
    group = lax.axis_index("blk")
    me = lax.axis_index("space")
    following = lax.rem(group + 1, blocks)
    preceding = lax.rem(group + blocks - 1, blocks)
    others = [j + (me <= j).astype(jnp.int32) for j in range(n - 1)]

    loads = [
        pltpu.make_async_copy(e_hbm.at[0], e_ref, load_sem.at[0]),
        pltpu.make_async_copy(h_hbm.at[0], h_ref, load_sem.at[1]),
        pltpu.make_async_copy(zf_hbm, zf_ref, load_sem.at[2]),
        pltpu.make_async_copy(chunk_hbm, chunk_ref, load_sem.at[3]),
        pltpu.make_async_copy(back_hbm, back_ref, load_sem.at[4]),
        pltpu.make_async_copy(tab_hbm, tab_ref, load_sem.at[5]),
    ]
    zi_ref = back_ref.at[0 : 2 * LANES]
    yi_ref = back_ref.at[2 * LANES : 3 * LANES]
    last = 2 * chunks - 2
    part = wide // 2
    pieces = [slice(last * part, last * part + part // 2), slice(last * part + part // 2, (last + 1) * part)]
    entries = [last, 2 * chunks]
    source, relay = blocks - 1, 2
    relayed = blocks > 4
    detour = group == (source if relayed else -1)
    onward = group == (relay if relayed else -1)

    def hole_copy(k):
        window = pl.ds(pl.multiple_of(k * part, part), part)
        return pltpu.make_async_remote_copy(
            src_ref=h_hbm.at[0, :, :, :, window], dst_ref=prev_ref.at[:, :, :, window],
            send_sem=hole_send.at[k], recv_sem=hole_recv.at[k],
            device_id=(following, me), device_id_type=MESH,
        )

    def piece_copy(i):
        return pltpu.make_async_remote_copy(
            src_ref=h_hbm.at[0, :, :, :, pieces[i]], dst_ref=prev_ref.at[:, :, :, pieces[i]],
            send_sem=hole_send.at[entries[i]], recv_sem=hole_recv.at[entries[i]],
            device_id=(following, me), device_id_type=MESH,
        )

    def detour_copy():
        return pltpu.make_async_remote_copy(
            src_ref=h_hbm.at[0, :, :, :, pieces[0]], dst_ref=relay_ref,
            send_sem=hole_send.at[entries[0]], recv_sem=relay_recv,
            device_id=(relay, me), device_id_type=MESH,
        )

    def onward_copy():
        return pltpu.make_async_remote_copy(
            src_ref=relay_ref, dst_ref=prev_ref.at[:, :, :, pieces[0]],
            send_sem=relay_send, recv_sem=hole_recv.at[entries[0]],
            device_id=(0, me), device_id_type=MESH,
        )

    swapping = blocks % 4 == 0
    asks = lax.rem(group, 4) == (0 if swapping else -1)
    answers = lax.rem(group, 4) == (3 if swapping else -1)

    def visit_copy():
        return pltpu.make_async_remote_copy(
            src_ref=e_hbm.at[0, :, :, :, pieces[1]], dst_ref=visit_ref,
            send_sem=swap_send.at[0], recv_sem=swap_recv.at[0],
            device_id=(preceding, me), device_id_type=MESH,
        )

    def answer_copy():
        return pltpu.make_async_remote_copy(
            src_ref=answer_ref, dst_ref=reply_ref,
            send_sem=swap_send.at[1], recv_sem=swap_recv.at[1],
            device_id=(following, me), device_id_type=MESH,
        )

    def start_holes():
        for k in range(last):
            hole_copy(k).start()
        pl.when(jnp.logical_not(detour))(piece_copy(0).start)
        pl.when(jnp.logical_not(answers))(piece_copy(1).start)
        hole_copy(last + 1).start()

    even = lax.rem(group, 2) == 0
    barrier = pltpu.get_barrier_semaphore()
    pl.semaphore_signal(barrier, inc=1, device_id=(preceding, me), device_id_type=MESH)

    if relayed:
        @pl.when(onward)
        def _():
            pl.semaphore_signal(barrier, inc=1, device_id=(source, me), device_id_type=MESH)

    @pl.when(even)
    def _():
        for other in others:
            pl.semaphore_signal(barrier, inc=1, device_id=(group, other), device_id_type=MESH)

    for copy in loads:
        copy.start()

    @pl.when(jnp.logical_not(even))
    def _():
        pl.semaphore_wait(barrier, jnp.where(detour, 2, 1))
        pl.when(detour)(detour_copy().start)
        start_holes()

    @pl.when(even)
    def _():
        pl.semaphore_wait(barrier, n)
        start_holes()
        for other in others:
            pl.semaphore_signal(greet_sem, inc=1, device_id=(group, other), device_id_type=MESH)
        pl.semaphore_wait(greet_sem, n - 1)
        pl.semaphore_signal(ready_sem, inc=1, device_id=(following, me), device_id_type=MESH)

    lane = lax.broadcasted_iota(jnp.int32, (1, LANES), 1)
    first_half = lane < LANES // 2
    sign = sign_of(lane)

    def products(electrons, e_window, holes, h_window):
        real = imag = None
        for b in range(bands):
            er = electrons[b, 0, :, e_window].astype(F32)
            ei = electrons[b, 1, :, e_window].astype(F32)
            hr = holes[b, 0, :, h_window].astype(F32)
            hi = holes[b, 1, :, h_window].astype(F32)
            if b == 0:
                real, imag = er * hr + ei * hi, er * hi - ei * hr
            else:
                real = real + (er * hr + ei * hi)
                imag = imag + (er * hi - ei * hr)
        return real, imag

    def place(t, real, imag):
        moved_real = pltpu.roll(real, LANES // 2, 1)
        moved_imag = pltpu.roll(imag, LANES // 2, 1)
        stage_ref[pl.ds(2 * t, rows, stride=CHUNK), :] = jnp.where(first_half, real, moved_imag)
        stage_ref[pl.ds(2 * t + 1, rows, stride=CHUNK), :] = jnp.where(first_half, moved_real, imag)

    def clear(c):
        @pl.loop(0, rows)
        def _(x):
            rho_ref[c, pl.ds(pl.multiple_of(x * ny, ny), ny), :] = jnp.zeros((ny, LANES), F32)

    def density(c, holes, k, tiles):
        for t in tiles:
            if c == 1 and t % (part // LANES) == 0:
                hole_copy(2 * k + t // (part // LANES)).wait_recv()
            window = pl.ds(pl.multiple_of(k * wide + t * LANES, LANES), LANES)
            place(t, *products(e_ref, window, holes, window))

    def last_density():
        piece_copy(0).wait_recv()
        place(0, *products(e_ref, pieces[0], prev_ref, pieces[0]))

        @pl.when(jnp.logical_not(asks))
        def _():
            piece_copy(1).wait_recv()
            place(1, *products(e_ref, pieces[1], prev_ref, pieces[1]))

        @pl.when(asks)
        def _():
            answer_copy().wait_recv()
            place(1, reply_ref[0], reply_ref[1])

        density(1, prev_ref, chunks - 1, range(2, 4))

    def absorb(c, holes, k):
        density(c, holes, k, range(wide // LANES))
        gather(c, k)

    def gather(c, k):
        high, low = split(stage_ref[...])
        both = jnp.dot(
            jnp.concatenate([high, low], 1), zf_ref[...], preferred_element_type=F32
        )
        deep = both[:, :LANES] + both[:, LANES:]
        turn = turned(deep, sign)
        table = chunk_ref[k][:, : 6 * CHUNK]
        for x in range(0, rows, 2):
            pair = []
            for j in (x, x + 1):
                own = slice(j * CHUNK, (j + 1) * CHUNK)
                pair.append(jnp.concatenate([deep[own], turn[own]], 0))
            high, low = split(jnp.concatenate(pair, 1))
            share = jnp.dot(
                table, jnp.concatenate([high, low, high], 0), preferred_element_type=F32
            )
            for j in range(2):
                own = slice((x + j) * ny, (x + j + 1) * ny)
                rho_ref[c, own, :] = rho_ref[c, own, :] + share[:, j * LANES : (j + 1) * LANES]

    planes = min(rows, 4)
    span = planes * ny
    block = 16

    fields = [fld_ref, out_ref]

    empty = jnp.zeros((block, LANES), F32)
    zero_row = jnp.zeros((1, LANES), F32)

    def sweep(c):
        def body(i, sums):
            energy, cross_real, cross_imag = sums
            at = pl.multiple_of(i * block, block)
            decay = tab_ref[0, pl.ds(at, block), :]
            response = tab_ref[1, pl.ds(at, block), :]
            left = right = empty
            spread = []
            for x in reversed(range(rows)):
                right = decay * right
                spread.append(right)
                right = right + rho_ref[c, pl.ds(x * ny + at, block), :]
            for x in range(rows):
                own = pl.ds(x * ny + at, block)
                value = rho_ref[c, own, :]
                left = decay * left + value
                field = response * (left + spread[rows - 1 - x])
                fields[c][own, :] = field
                energy = energy + field * value
                if c == 1:
                    cross_real = cross_real + fld_ref[own, :] * value
                    cross_imag = cross_imag + turn_ref[own, :] * value
            msg_ref[c, pl.ds(at, block), :] = left
            msg_ref[c, pl.ds(ny + at, block), :] = right
            return energy, cross_real, cross_imag

        sums = lax.fori_loop(0, ny // block, body, (empty,) * 3, unroll=4)
        total = rho_ref[c, 0:8, :]
        for x in range(1, rows):
            total = total + rho_ref[c, x * ny : x * ny + 8, :]
        tail = [total[0:1]] + [jnp.sum(part, axis=0, keepdims=True) for part in sums]
        msg_ref[c, 2 * ny : 2 * ny + 8, :] = jnp.concatenate(tail + [zero_row] * 4, 0)
        copies = []
        for j in range(n - 1):
            slot = lax.rem(others[j] - me - 1 + n, n)
            copies.append(
                pltpu.make_async_remote_copy(
                    src_ref=msg_ref.at[c], dst_ref=recv_ref.at[c, slot],
                    send_sem=msg_send.at[c, j], recv_sem=msg_recv.at[c, slot],
                    device_id=(group, others[j]), device_id_type=MESH,
                )
            )
        for copy in copies:
            copy.start()
        return copies

    def arrive(c):
        for k in range(n - 1):
            pltpu.make_async_remote_copy(
                src_ref=msg_ref.at[c], dst_ref=recv_ref.at[c, k],
                send_sem=msg_send.at[c, k], recv_sem=msg_recv.at[c, k],
                device_id=(group, others[k]), device_id_type=MESH,
            ).wait_recv()

    def tails(c, row):
        total = msg_ref[c, 2 * ny + row : 2 * ny + row + 1, :]
        for k in range(n - 1):
            total = total + recv_ref[c, k, 2 * ny + row : 2 * ny + row + 1, :]
        return total

    def solve(c):
        mean = tails(c, 0)

        def body(i, energy):
            at = pl.multiple_of(i * block, block)
            decay = tab_ref[0, pl.ds(at, block), :]
            response = tab_ref[1, pl.ds(at, block), :]
            background = tab_ref[2, pl.ds(at, block), :] * mean
            weights = [tab_ref[3 + k, pl.ds(at, block), :] for k in range(n)]
            rights = [msg_ref[c, pl.ds(at, block), :]]
            lefts = [msg_ref[c, pl.ds(ny + at, block), :]]
            for k in range(n - 1):
                rights.append(recv_ref[c, k, pl.ds(at, block), :])
                lefts.append(recv_ref[c, k, pl.ds(ny + at, block), :])
            left = right = pairs = empty
            for a in range(n):
                coming = empty
                for k in range(n):
                    coming = coming + weights[k] * rights[(a + k + 1) % n]
                pairs = pairs + coming * lefts[a]
                if a == 0:
                    left = coming
            for k in range(n):
                right = right + weights[k] * lefts[(n - k - 1) % n]
            energy = energy + 2.0 * response * decay * pairs - background * mean
            left = response * left
            right = response * right
            spread = []
            for x in range(rows):
                right = decay * right
                spread.append(right)
            for x in range(rows):
                left = decay * left
                own = pl.ds(x * ny + at, block)
                fields[c][own, :] = fields[c][own, :] + (
                    left + spread[rows - 1 - x] - background
                )
            return energy

        total = lax.fori_loop(0, ny // block, body, empty, unroll=4)
        return jnp.sum(total, axis=0, keepdims=True)

    for copy in loads:
        copy.wait()

    clear(0)
    clear(1)

    @pl.loop(0, chunks)
    def _(k):
        absorb(0, h_ref, k)

    @pl.when(jnp.logical_not(even))
    def _():
        pl.semaphore_wait(ready_sem, 1)

    copies0 = sweep(0)

    early = min(chunks, 2)

    @pl.loop(0, early)
    def _(k):
        absorb(1, prev_ref, k)

    pl.when(asks)(visit_copy().start)
    arrive(0)
    sum_ref[0:1, :] = tails(0, 1) + solve(0)

    @pl.loop(0, rows // planes)
    def _(i):
        own = pl.ds(pl.multiple_of(i * span, span), span)
        values = fld_ref[own, :]
        turn_ref[own, :] = turned(values, sign)
        res_ref[own, :] = inverse(values, zi_ref, yi_ref, ny, sign)

    @pl.when(answers)
    def _():
        visit_copy().wait_recv()
        real, imag = products(visit_ref, slice(None), h_ref, pieces[1])
        answer_ref[0] = real
        answer_ref[1] = imag
        answer_copy().start()

    if relayed:
        @pl.when(onward)
        def _():
            detour_copy().wait_recv()
            onward_copy().start()

    @pl.loop(early, chunks - 1)
    def _(k):
        absorb(1, prev_ref, k)

    last_density()
    gather(1, chunks - 1)

    copies1 = sweep(1)
    for k in range(last):
        hole_copy(k).wait_send()
    for copy in [hole_copy(last + 1), piece_copy(0)] + copies0:
        copy.wait_send()
    pl.when(jnp.logical_not(answers))(piece_copy(1).wait_send)
    pl.when(answers)(answer_copy().wait_send)
    pl.when(asks)(visit_copy().wait_send)
    if relayed:
        pl.when(onward)(onward_copy().wait_send)
    arrive(1)
    sum_ref[1:2, :] = tails(1, 1) + solve(1)
    sum_ref[2:3, :] = tails(1, 2)
    sum_ref[3:4, :] = tails(1, 3)
    sum_ref[4:8, :] = jnp.zeros((4, LANES), F32)

    for copy in copies1:
        copy.wait_send()


def finish(
    ny, scale, order_ref, res_ref, fld_ref, sum_ref, back_ref, out_hbm, coul_hbm,
    value_ref, entry_ref, sems,
):
    flat = res_ref.shape[0]
    first, second = order_ref[0:1, 0:1], order_ref[0:1, 1:2]
    spot = jnp.sum(first.astype(F32)).astype(jnp.int32)
    copies = [pltpu.make_async_copy(res_ref, out_hbm.at[spot], sems.at[0])]
    copies[0].start()
    sign = sign_of(lax.broadcasted_iota(jnp.int32, (1, LANES), 1))
    span = min(flat // ny, 4) * ny
    steps = flat // span
    for i in range(steps):
        own = slice(i * span, (i + 1) * span)
        value_ref[own, :] = inverse(
            fld_ref[own, :], back_ref.at[0 : 2 * LANES], back_ref.at[2 * LANES : 3 * LANES],
            ny, sign,
        )
        copies.append(
            pltpu.make_async_copy(value_ref.at[own], out_hbm.at[1 - spot, own], sems.at[1 + i])
        )
        copies[-1].start()
    entries = [jnp.sum(sum_ref[k : k + 1, :]) * scale for k in range(4)]
    shape = (2, 2, 2)
    part_of = lax.broadcasted_iota(jnp.int32, shape, 0)
    row = lax.broadcasted_iota(jnp.int32, shape, 1)
    column = lax.broadcasted_iota(jnp.int32, shape, 2)
    row_pair = jnp.where(row == 0, first[None], second[None])
    column_pair = jnp.where(column == 0, first[None], second[None])
    same = row_pair == column_pair
    opening = row_pair == 0
    real = jnp.where(same, jnp.where(opening, entries[0], entries[1]), entries[2])
    imag = jnp.where(same, 0.0, jnp.where(opening, entries[3], -entries[3]))
    entry_ref[0] = jnp.where(part_of == 0, real, imag)
    copies.append(pltpu.make_async_copy(entry_ref, coul_hbm, sems.at[1 + steps]))
    copies[-1].start()
    for copy in copies:
        copy.wait()


def shards(n, blocks, electrons, holes, pair_order):
    _, bands, parts, rows, cells = electrons.shape
    ny = nz = math.isqrt(cells)
    flat = rows * ny
    nx = rows * n
    vmem = pl.BlockSpec(memory_space=pltpu.VMEM)
    hbm = pl.BlockSpec(memory_space=pl.ANY)
    states = (bands, parts, rows, cells)
    message = 2 * ny + 8
    chunks = ny // CHUNK
    back = np.concatenate([depth_table(nz, -1.0), column_table(ny, -1.0)])
    tables = solver_tables(nx, ny, nz, n)
    stored, field, sums, back_kept = pl.pallas_call(
        functools.partial(kernel, n, blocks, ny),
        out_shape=(
            pltpu.VMEM((flat, LANES), F32),
            pltpu.VMEM((flat, LANES), F32),
            pltpu.VMEM((8, LANES), F32),
            pltpu.VMEM(back.shape, BF16),
        ),
        in_specs=[hbm] * 6,
        out_specs=(vmem,) * 4,
        scratch_shapes=[
            pltpu.VMEM(states, BF16),
            pltpu.VMEM(states, BF16),
            pltpu.VMEM(states, BF16),
            pltpu.VMEM((rows * CHUNK, LANES), F32),
            pltpu.VMEM((2, flat, LANES), F32),
            pltpu.VMEM((flat, LANES), F32),
            pltpu.VMEM((2, message, LANES), F32),
            pltpu.VMEM((2, n - 1, message, LANES), F32),
            pltpu.VMEM((flat, LANES), F32),
            pltpu.VMEM((bands, parts, rows, LANES), BF16),
            pltpu.VMEM((bands, parts, rows, LANES), BF16),
            pltpu.VMEM((2, rows, LANES), F32),
            pltpu.VMEM((2, rows, LANES), F32),
            pltpu.VMEM((2 * LANES, 2 * LANES), BF16),
            pltpu.VMEM((chunks, ny, LANES), BF16),
            pltpu.VMEM(tables.shape, F32),
            pltpu.SemaphoreType.DMA((6,)),
            pltpu.SemaphoreType.DMA((2 * chunks + 1,)),
            pltpu.SemaphoreType.DMA((2 * chunks + 1,)),
            pltpu.SemaphoreType.DMA((2, n - 1)),
            pltpu.SemaphoreType.DMA((2, n - 1)),
            pltpu.SemaphoreType.DMA,
            pltpu.SemaphoreType.DMA,
            pltpu.SemaphoreType.DMA((2,)),
            pltpu.SemaphoreType.DMA((2,)),
            pltpu.SemaphoreType.REGULAR,
            pltpu.SemaphoreType.REGULAR,
        ],
        compiler_params=pltpu.CompilerParams(
            collective_id=0, has_side_effects=True, vmem_limit_bytes=60 * 2**20
        ),
        name="screened",
    )(
        electrons,
        holes,
        jnp.asarray(depth_table(nz, 1.0)),
        jnp.asarray(chunk_table(ny)),
        jnp.asarray(back),
        jnp.asarray(tables),
    )
    potential, coulomb = pl.pallas_call(
        functools.partial(finish, ny, 1.0 / (nx * cells)),
        out_shape=(
            jax.ShapeDtypeStruct((2, flat, LANES), F32),
            jax.ShapeDtypeStruct((1, 2, 2, 2), F32),
        ),
        in_specs=[vmem] * 5,
        out_specs=(hbm, hbm),
        scratch_shapes=[
            pltpu.VMEM((flat, LANES), F32),
            pltpu.VMEM((1, 2, 2, 2), F32),
            pltpu.SemaphoreType.DMA((2 + flat // (min(rows, 4) * ny),)),
        ],
        compiler_params=pltpu.CompilerParams(vmem_limit_bytes=16 * 2**20),
        name="finish",
    )(pair_order, stored, field, sums, back_kept)
    return potential.reshape(1, 2, rows, ny, 2 * nz), coulomb


def solution(mesh):
    body = functools.partial(shards, mesh.shape["space"], mesh.shape["blk"])
    in_specs = (
        P("blk", None, None, "space", None),
        P("blk", None, None, "space", None),
        P("blk", None),
    )
    out_specs = (P("blk", None, "space", None, None), P("blk", None, None, None))
    return jax.shard_map(body, mesh=mesh, in_specs=in_specs, out_specs=out_specs, check_vma=False)
```

```python
import functools
import math

import jax
import jax.numpy as jnp
import numpy as np
from jax import lax
from jax.experimental import pallas as pl
from jax.experimental.pallas import tpu as pltpu
from jax.sharding import PartitionSpec as P

SCREENING = 0.01
MESH = pl.DeviceIdType.MESH
LANES = 128
CHUNK = 8
F32 = jnp.float32
BF16 = jnp.bfloat16


def halves(matrix):
    high = matrix.astype(jnp.bfloat16)
    low = (matrix - high.astype(np.float64)).astype(jnp.bfloat16)
    return high, low


def phases(points):
    positions = np.arange(points)
    angles = 2.0 * math.pi / points * (np.outer(positions, positions) % points)
    return np.cos(angles), np.sin(angles)


def depth_table(points, direction):
    cosines, sines = phases(points)
    sines = direction * sines
    matrix = np.concatenate(
        [np.concatenate([cosines, -sines], 1), np.concatenate([sines, cosines], 1)], 0
    )
    high, low = halves(matrix)
    top = np.concatenate([high, low], 1)
    bottom = np.concatenate([high, np.zeros_like(high)], 1)
    return np.concatenate([top, bottom], 0)


def column_table(points, direction):
    cosines, sines = phases(points)
    high, low = halves(np.concatenate([cosines, direction * sines], 1))
    top = np.concatenate([high, high], 1)
    bottom = np.concatenate([low, np.zeros_like(low)], 1)
    return np.concatenate([top, bottom], 0)


def chunk_table(points):
    cosines, sines = phases(points)
    tables = []
    for start in range(0, points, CHUNK):
        own = slice(start, start + CHUNK)
        high, low = halves(np.concatenate([cosines[:, own], sines[:, own]], 1))
        fill = np.zeros((points, LANES - 6 * CHUNK), high.dtype)
        tables.append(np.concatenate([high, high, low, fill], 1))
    return np.stack(tables)


def solver_tables(nx, ny, nz, devices):
    term_y = 2.0 - 2.0 * np.cos(2.0 * math.pi / ny * np.arange(ny))
    term_z = 2.0 - 2.0 * np.cos(2.0 * math.pi / nz * (np.arange(2 * nz) % nz))
    shift = term_y[:, None] + term_z[None, :] + SCREENING
    root = np.sqrt(shift * (shift + 4.0))
    decay = 2.0 / (shift + 2.0 + root)
    response = 1.0 / root / (ny * nz)
    anchor = np.zeros_like(shift)
    anchor[0, 0] = anchor[0, nz] = 1.0 / (SCREENING * nx * ny * nz)
    rows = nx // devices
    weights = [decay ** (rows * j) / (1.0 - decay**nx) for j in range(devices)]
    return np.stack([decay, response, anchor] + weights).astype(np.float32)


def split(values):
    high = values.astype(BF16)
    return high, (values - high.astype(F32)).astype(BF16)


def turned(values, sign):
    return pltpu.roll(values, LANES // 2, values.ndim - 1) * sign


def sign_of(lane):
    return jnp.where(lane < LANES // 2, 1.0, -1.0).astype(F32)


def inverse(values, z_ref, y_ref, ny, sign):
    planes = values.shape[0] // ny
    high, low = split(values)
    wide = jnp.dot(jnp.concatenate([high, low], 1), z_ref[...], preferred_element_type=F32)
    deep = wide[:, :LANES] + wide[:, LANES:]
    turn = turned(deep, sign)
    high, low = split(deep)
    turn_high, turn_low = split(turn)
    parts = []
    for x in range(0, planes, 2):
        columns = []
        for k in (x, x + 1):
            own = slice(k * ny, (k + 1) * ny)
            columns.append(
                jnp.concatenate([high[own], turn_high[own], low[own], turn_low[own]], 0)
            )
        both = jnp.dot(y_ref[...], jnp.concatenate(columns, 1), preferred_element_type=F32)
        total = both[:ny] + both[ny:]
        parts += [total[:, :LANES], total[:, LANES:]]
    return jnp.concatenate(parts, 0)


def kernel(
    n, blocks, ny,
    e_hbm, h_hbm, zf_hbm, chunk_hbm, back_hbm, tab_hbm,
    res_ref, out_ref, sum_ref, back_ref,
    e_ref, h_ref, prev_ref, stage_ref, rho_ref, fld_ref, msg_ref, recv_ref,
    part_ref, peer_ref, turn_ref, relay_ref, visit_ref, answer_ref, reply_ref, zf_ref, chunk_ref, tab_ref,
    load_sem, hole_send, hole_recv, msg_send, msg_recv, part_send, part_recv, relay_send, relay_recv, swap_send, swap_recv, greet_sem, ready_sem,
):
    bands, _, rows, cells = e_ref.shape
    chunks = ny // CHUNK
    wide = cells // chunks
    group = lax.axis_index("blk")
    me = lax.axis_index("space")
    following = lax.rem(group + 1, blocks)
    preceding = lax.rem(group + blocks - 1, blocks)
    others, low, high = [], 0, n - 1
    for _ in range(n - 1):
        below = (me - low >= high - me).astype(jnp.int32)
        others.append(below * low + (1 - below) * high)
        low, high = low + below, high - 1 + below

    loads = [
        pltpu.make_async_copy(e_hbm.at[0], e_ref, load_sem.at[0]),
        pltpu.make_async_copy(h_hbm.at[0], h_ref, load_sem.at[1]),
        pltpu.make_async_copy(zf_hbm, zf_ref, load_sem.at[2]),
        pltpu.make_async_copy(chunk_hbm, chunk_ref, load_sem.at[3]),
        pltpu.make_async_copy(back_hbm, back_ref, load_sem.at[4]),
        pltpu.make_async_copy(tab_hbm, tab_ref, load_sem.at[5]),
    ]
    zi_ref = back_ref.at[0 : 2 * LANES]
    yi_ref = back_ref.at[2 * LANES : 3 * LANES]
    last = 2 * chunks - 2
    part = wide // 2
    pieces = [slice(last * part, last * part + part // 2), slice(last * part + part // 2, (last + 1) * part)]
    entries = [last, 2 * chunks]
    source, relay = blocks - 1, 2
    relayed = blocks > 4 and n % 2 == 0
    detour = group == (source if relayed else -1)
    onward = group == (relay if relayed else -1)
    mirror = n - 1 - me
    above = 0

    def hole_copy(k):
        window = pl.ds(pl.multiple_of(k * part, part), part)
        return pltpu.make_async_remote_copy(
            src_ref=h_hbm.at[0, :, :, :, window], dst_ref=prev_ref.at[:, :, :, window],
            send_sem=hole_send.at[k], recv_sem=hole_recv.at[k],
            device_id=(following, me), device_id_type=MESH,
        )

    def piece_copy(i):
        return pltpu.make_async_remote_copy(
            src_ref=h_hbm.at[0, :, :, :, pieces[i]], dst_ref=prev_ref.at[:, :, :, pieces[i]],
            send_sem=hole_send.at[entries[i]], recv_sem=hole_recv.at[entries[i]],
            device_id=(following, me), device_id_type=MESH,
        )

    def detour_copy(slot):
        return pltpu.make_async_remote_copy(
            src_ref=h_hbm.at[0, :, :, :, pieces[0]], dst_ref=relay_ref.at[slot],
            send_sem=hole_send.at[entries[0]], recv_sem=relay_recv.at[slot],
            device_id=(relay, me), device_id_type=MESH,
        )

    def onward_copy(slot):
        return pltpu.make_async_remote_copy(
            src_ref=relay_ref.at[slot], dst_ref=prev_ref.at[:, :, :, pieces[0]],
            send_sem=relay_send.at[slot], recv_sem=hole_recv.at[entries[0]],
            device_id=(0, mirror if slot else me), device_id_type=MESH,
        )

    swapping = blocks % 4 == 0
    asks = lax.rem(group, 4) == (0 if swapping else -1)
    answers = lax.rem(group, 4) == (3 if swapping else -1)

    def visit_copy():
        return pltpu.make_async_remote_copy(
            src_ref=e_hbm.at[0, :, :, :, pieces[1]], dst_ref=visit_ref,
            send_sem=swap_send.at[0], recv_sem=swap_recv.at[0],
            device_id=(preceding, me), device_id_type=MESH,
        )

    def answer_copy():
        return pltpu.make_async_remote_copy(
            src_ref=answer_ref, dst_ref=reply_ref,
            send_sem=swap_send.at[1], recv_sem=swap_recv.at[1],
            device_id=(following, me), device_id_type=MESH,
        )

    opening = min(8, last)

    def open_holes():
        for k in range(opening):
            hole_copy(k).start()

    def close_holes():
        for k in range(opening, last):
            hole_copy(k).start()
        pl.when(jnp.logical_not(detour))(piece_copy(0).start)
        pl.when(jnp.logical_not(answers))(piece_copy(1).start)
        hole_copy(last + 1).start()

    even = lax.rem(group, 2) == 0
    barrier = pltpu.get_barrier_semaphore()
    pl.semaphore_signal(barrier, inc=1, device_id=(preceding, me), device_id_type=MESH)

    if relayed:
        @pl.when(group == relay)
        def _():
            pl.semaphore_signal(barrier, inc=1, device_id=(source - 1, me), device_id_type=MESH)

    @pl.when(even)
    def _():
        for other in others:
            pl.semaphore_signal(barrier, inc=1, device_id=(group, other), device_id_type=MESH)

    for copy in loads:
        copy.start()

    @pl.when(jnp.logical_not(even))
    def _():
        pl.semaphore_wait(barrier, 1)
        open_holes()

    @pl.when(even)
    def _():
        pl.semaphore_wait(barrier, n + (group == source - 1).astype(jnp.int32) if relayed else n)
        open_holes()
        close_holes()
        for other in others:
            pl.semaphore_signal(greet_sem, inc=1, device_id=(group, other), device_id_type=MESH)
        pl.semaphore_wait(greet_sem, n - 1)
        pl.semaphore_signal(ready_sem, inc=1, device_id=(following, me), device_id_type=MESH)

    lane = lax.broadcasted_iota(jnp.int32, (1, LANES), 1)
    first_half = lane < LANES // 2
    sign = sign_of(lane)

    def products(electrons, e_window, holes, h_window):
        real = imag = None
        for b in range(bands):
            er = electrons[b, 0, :, e_window].astype(F32)
            ei = electrons[b, 1, :, e_window].astype(F32)
            hr = holes[b, 0, :, h_window].astype(F32)
            hi = holes[b, 1, :, h_window].astype(F32)
            if b == 0:
                real, imag = er * hr + ei * hi, er * hi - ei * hr
            else:
                real = real + (er * hr + ei * hi)
                imag = imag + (er * hi - ei * hr)
        return real, imag

    def place(t, real, imag):
        moved_real = pltpu.roll(real, LANES // 2, 1)
        moved_imag = pltpu.roll(imag, LANES // 2, 1)
        stage_ref[pl.ds(2 * t, rows, stride=CHUNK), :] = jnp.where(first_half, real, moved_imag)
        stage_ref[pl.ds(2 * t + 1, rows, stride=CHUNK), :] = jnp.where(first_half, moved_real, imag)

    def clear(c):
        @pl.loop(0, rows)
        def _(x):
            rho_ref[c, pl.ds(pl.multiple_of(x * ny, ny), ny), :] = jnp.zeros((ny, LANES), F32)

    def density(c, holes, k, tiles):
        for t in tiles:
            if c == 1 and t % (part // LANES) == 0:
                hole_copy(2 * k + t // (part // LANES)).wait_recv()
            window = pl.ds(pl.multiple_of(k * wide + t * LANES, LANES), LANES)
            place(t, *products(e_ref, window, holes, window))

    def last_density():
        piece_copy(0).wait_recv()
        place(0, *products(e_ref, pieces[0], prev_ref, pieces[0]))

        @pl.when(jnp.logical_not(asks))
        def _():
            piece_copy(1).wait_recv()
            place(1, *products(e_ref, pieces[1], prev_ref, pieces[1]))

        @pl.when(asks)
        def _():
            answer_copy().wait_recv()
            place(1, reply_ref[0], reply_ref[1])

        density(1, prev_ref, chunks - 1, range(2, 4))

    def absorb(c, holes, k):
        density(c, holes, k, range(wide // LANES))
        gather(c, k)

    def gather(c, k, closing=False):
        high, low = split(stage_ref[...])
        both = jnp.dot(
            jnp.concatenate([high, low], 1), zf_ref[...], preferred_element_type=F32
        )
        deep = both[:, :LANES] + both[:, LANES:]
        turn = turned(deep, sign)
        table = chunk_ref[k][:, : 6 * CHUNK]
        if closing:
            decay = tab_ref[0]
            left = right = jnp.zeros((ny, LANES), F32)
            power = None
        for x in range(0, rows, 2):
            pair = []
            for j in (x, x + 1):
                own = slice(j * CHUNK, (j + 1) * CHUNK)
                pair.append(jnp.concatenate([deep[own], turn[own]], 0))
            high, low = split(jnp.concatenate(pair, 1))
            share = jnp.dot(
                table, jnp.concatenate([high, low, high], 0), preferred_element_type=F32
            )
            for j in range(2):
                own = slice((x + j) * ny, (x + j + 1) * ny)
                value = share[:, j * LANES : (j + 1) * LANES]
                rho_ref[c, own, :] = rho_ref[c, own, :] + value
                if closing:
                    left = value if power is None else decay * left + value
                    right = value if power is None else right + power * value
                    power = decay if power is None else power * decay
        if closing:
            msg_ref[c, 0:ny, :] = msg_ref[c, 0:ny, :] + left
            msg_ref[c, ny : 2 * ny, :] = msg_ref[c, ny : 2 * ny, :] + right

    planes = min(rows, 4)
    span = planes * ny
    block = 16

    fields = [fld_ref, out_ref]

    empty = jnp.zeros((block, LANES), F32)
    zero_row = jnp.zeros((1, LANES), F32)

    def sweep(c):
        def body(i, sums):
            energy, cross_real, cross_imag = sums
            at = pl.multiple_of(i * block, block)
            decay = tab_ref[0, pl.ds(at, block), :]
            response = tab_ref[1, pl.ds(at, block), :]
            left = right = empty
            spread = []
            for x in reversed(range(rows)):
                right = decay * right
                spread.append(right)
                right = right + rho_ref[c, pl.ds(x * ny + at, block), :]
            for x in range(rows):
                own = pl.ds(x * ny + at, block)
                value = rho_ref[c, own, :]
                left = decay * left + value
                field = response * (left + spread[rows - 1 - x])
                fields[c][own, :] = field
                energy = energy + field * value
                if c == 1:
                    cross_real = cross_real + fld_ref[own, :] * value
                    cross_imag = cross_imag + turn_ref[own, :] * value
            if c == 0:
                msg_ref[c, pl.ds(at, block), :] = left
                msg_ref[c, pl.ds(ny + at, block), :] = right
            return energy, cross_real, cross_imag

        sums = lax.fori_loop(0, ny // block, body, (empty,) * 3, unroll=4)
        rest = [jnp.sum(part, axis=0, keepdims=True) for part in sums]
        rest = jnp.concatenate(rest + [zero_row] * 4, 0)
        if c == 0:
            msg_ref[c, 2 * ny : 2 * ny + 8, :] = jnp.concatenate([mean_row(c), rest], 0)
        else:
            part_ref[...] = jnp.concatenate([mean_row(c), rest], 0)

    def mean_row(c):
        total = rho_ref[c, 0:8, :]
        for x in range(1, rows):
            total = total + rho_ref[c, x * ny : x * ny + 8, :]
        return total[0:1]

    def moments(c):
        def body(i, carry):
            at = pl.multiple_of(i * block, block)
            decay = tab_ref[0, pl.ds(at, block), :]
            left = right = empty
            for x in range(rows):
                left = decay * left + rho_ref[c, pl.ds(x * ny + at, block), :]
                right = decay * right + rho_ref[c, pl.ds((rows - 1 - x) * ny + at, block), :]
            msg_ref[c, pl.ds(at, block), :] = left
            msg_ref[c, pl.ds(ny + at, block), :] = right
            return carry

        lax.fori_loop(0, ny // block, body, 0)

    def message_rows(c):
        return 2 * ny + (8 if c == 0 else 0)

    def message_copies(c):
        copies = []
        for j in range(n - 1):
            slot = lax.rem(others[j] - me - 1 + n, n)
            copies.append(
                pltpu.make_async_remote_copy(
                    src_ref=msg_ref.at[c, : message_rows(c)], dst_ref=recv_ref.at[c, slot, : message_rows(c)],
                    send_sem=msg_send.at[c, j], recv_sem=msg_recv.at[c, slot],
                    device_id=(group, others[j]), device_id_type=MESH,
                )
            )
        return copies

    def part_copies():
        copies = []
        for j in range(n - 1):
            slot = lax.rem(others[j] - me - 1 + n, n)
            copies.append(
                pltpu.make_async_remote_copy(
                    src_ref=part_ref, dst_ref=peer_ref.at[slot],
                    send_sem=part_send.at[j], recv_sem=part_recv.at[slot],
                    device_id=(group, others[j]), device_id_type=MESH,
                )
            )
        return copies

    def arrive(c):
        for k in range(n - 1):
            pltpu.make_async_remote_copy(
                src_ref=msg_ref.at[c, : message_rows(c)], dst_ref=recv_ref.at[c, k, : message_rows(c)],
                send_sem=msg_send.at[c, k], recv_sem=msg_recv.at[c, k],
                device_id=(group, others[k]), device_id_type=MESH,
            ).wait_recv()

    def tails(c, row):
        total = msg_ref[c, 2 * ny + row : 2 * ny + row + 1, :]
        for k in range(n - 1):
            total = total + recv_ref[c, k, 2 * ny + row : 2 * ny + row + 1, :]
        return total

    def solve(c, mean):

        def body(i, energy):
            at = pl.multiple_of(i * block, block)
            decay = tab_ref[0, pl.ds(at, block), :]
            response = tab_ref[1, pl.ds(at, block), :]
            background = tab_ref[2, pl.ds(at, block), :] * mean
            weights = [tab_ref[3 + k, pl.ds(at, block), :] for k in range(n)]
            rights = [msg_ref[c, pl.ds(at, block), :]]
            lefts = [msg_ref[c, pl.ds(ny + at, block), :]]
            for k in range(n - 1):
                rights.append(recv_ref[c, k, pl.ds(at, block), :])
                lefts.append(recv_ref[c, k, pl.ds(ny + at, block), :])
            left = right = pairs = empty
            for a in range(n):
                coming = empty
                for k in range(n):
                    coming = coming + weights[k] * rights[(a + k + 1) % n]
                pairs = pairs + coming * lefts[a]
                if a == 0:
                    left = coming
            for k in range(n):
                right = right + weights[k] * lefts[(n - k - 1) % n]
            energy = energy + 2.0 * response * decay * pairs - background * mean
            left = response * left
            right = response * right
            spread = []
            for x in range(rows):
                right = decay * right
                spread.append(right)
            for x in range(rows):
                left = decay * left
                own = pl.ds(x * ny + at, block)
                fields[c][own, :] = fields[c][own, :] + (
                    left + spread[rows - 1 - x] - background
                )
            return energy

        total = lax.fori_loop(0, ny // block, body, empty, unroll=4)
        return jnp.sum(total, axis=0, keepdims=True)

    for copy in loads:
        copy.wait()

    clear(0)
    clear(1)

    @pl.loop(0, chunks)
    def _(k):
        absorb(0, h_ref, k)

    @pl.when(jnp.logical_not(even))
    def _():
        pl.semaphore_wait(ready_sem, 1)
        if relayed:
            pl.when(detour)(detour_copy(above).start)
        close_holes()

    sweep(0)
    copies0 = message_copies(0)
    for copy in copies0:
        copy.start()

    early = min(chunks, 2)

    @pl.loop(0, early)
    def _(k):
        absorb(1, prev_ref, k)

    pl.when(asks)(visit_copy().start)
    arrive(0)
    sum_ref[0:1, :] = tails(0, 1) + solve(0, tails(0, 0))

    @pl.loop(0, rows // planes)
    def _(i):
        own = pl.ds(pl.multiple_of(i * span, span), span)
        values = fld_ref[own, :]
        turn_ref[own, :] = turned(values, sign)
        res_ref[own, :] = inverse(values, zi_ref, yi_ref, ny, sign)

    @pl.when(answers)
    def _():
        visit_copy().wait_recv()
        real, imag = products(visit_ref, slice(None), h_ref, pieces[1])
        answer_ref[0] = real
        answer_ref[1] = imag
        answer_copy().start()

    if relayed:
        @pl.when(onward)
        def _():
            for slot in range(1):
                detour_copy(slot).wait_recv()
                onward_copy(slot).start()

    @pl.loop(early, chunks - 1)
    def _(k):
        absorb(1, prev_ref, k)

    moments(1)
    last_density()
    gather(1, chunks - 1, closing=True)
    copies1 = message_copies(1)
    copies1[0].start()
    sweep(1)
    copies2 = part_copies()
    for copy in copies2 + copies1[1:]:
        copy.start()
    for k in range(last):
        hole_copy(k).wait_send()
    for copy in [hole_copy(last + 1), piece_copy(0)] + copies0:
        copy.wait_send()
    pl.when(jnp.logical_not(answers))(piece_copy(1).wait_send)
    pl.when(answers)(answer_copy().wait_send)
    pl.when(asks)(visit_copy().wait_send)
    if relayed:
        @pl.when(onward)
        def _():
            for slot in range(1):
                onward_copy(slot).wait_send()
    arrive(1)
    for k in range(n - 1):
        pltpu.make_async_remote_copy(
            src_ref=part_ref, dst_ref=peer_ref.at[k],
            send_sem=part_send.at[k], recv_sem=part_recv.at[k],
            device_id=(group, others[k]), device_id_type=MESH,
        ).wait_recv()
    total = part_ref[...]
    for k in range(n - 1):
        total = total + peer_ref[k]
    sum_ref[1:2, :] = total[1:2] + solve(1, total[0:1])
    sum_ref[2:8, :] = total[2:8]

    for copy in copies1 + copies2:
        copy.wait_send()


def finish(
    ny, scale, order_ref, res_ref, fld_ref, sum_ref, back_ref, out_hbm, coul_hbm,
    value_ref, entry_ref, sems,
):
    flat = res_ref.shape[0]
    first, second = order_ref[0:1, 0:1], order_ref[0:1, 1:2]
    spot = jnp.sum(first.astype(F32)).astype(jnp.int32)
    copies = [pltpu.make_async_copy(res_ref, out_hbm.at[spot], sems.at[0])]
    copies[0].start()
    sign = sign_of(lax.broadcasted_iota(jnp.int32, (1, LANES), 1))
    span = min(flat // ny, 4) * ny
    steps = flat // span
    for i in range(steps):
        own = slice(i * span, (i + 1) * span)
        value_ref[own, :] = inverse(
            fld_ref[own, :], back_ref.at[0 : 2 * LANES], back_ref.at[2 * LANES : 3 * LANES],
            ny, sign,
        )
        copies.append(
            pltpu.make_async_copy(value_ref.at[own], out_hbm.at[1 - spot, own], sems.at[1 + i])
        )
        copies[-1].start()
    entries = [jnp.sum(sum_ref[k : k + 1, :]) * scale for k in range(4)]
    shape = (2, 2, 2)
    part_of = lax.broadcasted_iota(jnp.int32, shape, 0)
    row = lax.broadcasted_iota(jnp.int32, shape, 1)
    column = lax.broadcasted_iota(jnp.int32, shape, 2)
    row_pair = jnp.where(row == 0, first[None], second[None])
    column_pair = jnp.where(column == 0, first[None], second[None])
    same = row_pair == column_pair
    opening = row_pair == 0
    real = jnp.where(same, jnp.where(opening, entries[0], entries[1]), entries[2])
    imag = jnp.where(same, 0.0, jnp.where(opening, entries[3], -entries[3]))
    entry_ref[0] = jnp.where(part_of == 0, real, imag)
    copies.append(pltpu.make_async_copy(entry_ref, coul_hbm, sems.at[1 + steps]))
    copies[-1].start()
    for copy in copies:
        copy.wait()


def shards(n, blocks, electrons, holes, pair_order):
    _, bands, parts, rows, cells = electrons.shape
    ny = nz = math.isqrt(cells)
    flat = rows * ny
    nx = rows * n
    vmem = pl.BlockSpec(memory_space=pltpu.VMEM)
    hbm = pl.BlockSpec(memory_space=pl.ANY)
    states = (bands, parts, rows, cells)
    message = 2 * ny + 8
    chunks = ny // CHUNK
    back = np.concatenate([depth_table(nz, -1.0), column_table(ny, -1.0)])
    tables = solver_tables(nx, ny, nz, n)
    stored, field, sums, back_kept = pl.pallas_call(
        functools.partial(kernel, n, blocks, ny),
        out_shape=(
            pltpu.VMEM((flat, LANES), F32),
            pltpu.VMEM((flat, LANES), F32),
            pltpu.VMEM((8, LANES), F32),
            pltpu.VMEM(back.shape, BF16),
        ),
        in_specs=[hbm] * 6,
        out_specs=(vmem,) * 4,
        scratch_shapes=[
            pltpu.VMEM(states, BF16),
            pltpu.VMEM(states, BF16),
            pltpu.VMEM(states, BF16),
            pltpu.VMEM((rows * CHUNK, LANES), F32),
            pltpu.VMEM((2, flat, LANES), F32),
            pltpu.VMEM((flat, LANES), F32),
            pltpu.VMEM((2, message, LANES), F32),
            pltpu.VMEM((2, n - 1, message, LANES), F32),
            pltpu.VMEM((8, LANES), F32),
            pltpu.VMEM((n - 1, 8, LANES), F32),
            pltpu.VMEM((flat, LANES), F32),
            pltpu.VMEM((2, bands, parts, rows, LANES), BF16),
            pltpu.VMEM((bands, parts, rows, LANES), BF16),
            pltpu.VMEM((2, rows, LANES), F32),
            pltpu.VMEM((2, rows, LANES), F32),
            pltpu.VMEM((2 * LANES, 2 * LANES), BF16),
            pltpu.VMEM((chunks, ny, LANES), BF16),
            pltpu.VMEM(tables.shape, F32),
            pltpu.SemaphoreType.DMA((6,)),
            pltpu.SemaphoreType.DMA((2 * chunks + 1,)),
            pltpu.SemaphoreType.DMA((2 * chunks + 1,)),
            pltpu.SemaphoreType.DMA((2, n - 1)),
            pltpu.SemaphoreType.DMA((2, n - 1)),
            pltpu.SemaphoreType.DMA((n - 1,)),
            pltpu.SemaphoreType.DMA((n - 1,)),
            pltpu.SemaphoreType.DMA((2,)),
            pltpu.SemaphoreType.DMA((2,)),
            pltpu.SemaphoreType.DMA((2,)),
            pltpu.SemaphoreType.DMA((2,)),
            pltpu.SemaphoreType.REGULAR,
            pltpu.SemaphoreType.REGULAR,
        ],
        compiler_params=pltpu.CompilerParams(
            collective_id=0, has_side_effects=True, vmem_limit_bytes=60 * 2**20
        ),
        name="screened",
    )(
        electrons,
        holes,
        jnp.asarray(depth_table(nz, 1.0)),
        jnp.asarray(chunk_table(ny)),
        jnp.asarray(back),
        jnp.asarray(tables),
    )
    potential, coulomb = pl.pallas_call(
        functools.partial(finish, ny, 1.0 / (nx * cells)),
        out_shape=(
            jax.ShapeDtypeStruct((2, flat, LANES), F32),
            jax.ShapeDtypeStruct((1, 2, 2, 2), F32),
        ),
        in_specs=[vmem] * 5,
        out_specs=(hbm, hbm),
        scratch_shapes=[
            pltpu.VMEM((flat, LANES), F32),
            pltpu.VMEM((1, 2, 2, 2), F32),
            pltpu.SemaphoreType.DMA((2 + flat // (min(rows, 4) * ny),)),
        ],
        compiler_params=pltpu.CompilerParams(vmem_limit_bytes=16 * 2**20),
        name="finish",
    )(pair_order, stored, field, sums, back_kept)
    return potential.reshape(1, 2, rows, ny, 2 * nz), coulomb


def solution(mesh):
    body = functools.partial(shards, mesh.shape["space"], mesh.shape["blk"])
    in_specs = (
        P("blk", None, None, "space", None),
        P("blk", None, None, "space", None),
        P("blk", None),
    )
    out_specs = (P("blk", None, "space", None, None), P("blk", None, None, None))
    return jax.shard_map(body, mesh=mesh, in_specs=in_specs, out_specs=out_specs, check_vma=False)
```
